256 devices in a mesh: grp: 16 (over x, z_lo, core), row: 4 (over z_hi), col: 4 (over y).
Axes of the slice: x: 4, y: 4, z: 8 (z_hi: 4, z_lo: 2; z = z_hi * 2 + z_lo), core: 2. Of those that a mesh axis runs over, the one named last changes fastest.
Arguments:
- volume: float32 [32, 32, 32, 512], P(None, 'grp', 'row', 'col'), may hold values from -6 to 6
- forcing: float32 [32, 32, 32, 512], P(None, 'grp', 'row', 'col'), may hold values from -6 to 6
- medium: float32 [2, 32, 32, 512], P(None, 'grp', 'row', 'col'), may hold values from 0.5 to 3
- points: float32 [3, 32768], P(None, ('grp', 'row', 'col')), may hold values from 0 to 4
- weights: float32 [32768], P(('grp', 'row', 'col')), may hold values from 0.05 to 0.5
- cell_map: int32 [32768], P(('grp', 'row', 'col')), may hold values from 0 to 2047
- near_list: int32 [256, 256], replicated, may hold values from 0 to 1, as said below
Outputs:
- new_volume: float32 [32, 32, 32, 512], P(None, 'grp', 'row', 'col')
- potential: float32 [32, 32768], P(None, ('grp', 'row', 'col'))
The draws below stay inside these ranges and needn't reach their ends.
Inputs may be any that keep to these rules, and one draw needn't show every extreme that they name: cell_map[p] numbers a cell of tile p // 128 in row-major order of the tile's 2 x 8 x 128 cells. near_list[i, j] = 1 lists cluster j as near to cluster i; every cluster lists itself, and how many clusters a cluster lists differs from cluster to cluster.
All inputs are finite; a program needn't handle non-finite values.
Results may differ from the reference program's by a relative error of at most 0.0041.
Values may be sent and summed in bfloat16 or wider, within the bound.
No kernel may reach another device: no remote copies, remote signals or barrier semaphores. Data moves between devices by JAX's collectives and lax.ppermute only.
A program may use at most 64 MiB of HBM per device.

```python
import math
import jax
import jax.numpy as jnp
from jax import lax

RHS = 16
B_DEV = 128
CX = 2
CY = 8
CZ = 128
TY = 4
TZ = 4
TILES = 256
NX = 32
NY = 32
NZ = 512
POINTS = 32768
CH = 32


def draw_near_list(key, part):
    level_key = jax.random.fold_in(key, 11)
    pick_key = jax.random.fold_in(key, 12)
    levels = jax.random.randint(level_key, (TILES, 1), 1, 9)
    picks = jax.random.randint(pick_key, (TILES, TILES), 0, 8)
    listed = (picks < levels).astype(jnp.int32)
    rows_iota = lax.broadcasted_iota(jnp.int32, (TILES, TILES), 0)
    cols_iota = lax.broadcasted_iota(jnp.int32, (TILES, TILES), 1)
    diagonal = (rows_iota == cols_iota).astype(jnp.int32)
    return jnp.maximum(listed, diagonal)


def plant(values, stream_key, smallest, top_value):
    longest = values.shape.index(max(values.shape))
    spots = []
    for shift in (0, 1):
        where = [jax.random.randint(jax.random.fold_in(stream_key, axis), (), 0, length) for axis, length in enumerate(values.shape)]
        where[longest] = (where[longest] + shift) % values.shape[longest]
        spots.append(tuple(where))
    return values.at[spots[0]].set(smallest).at[spots[1]].set(top_value)


def block_scale(stream_key, extent, split, least, largest):
    def one(dim, parts):
        draws = jax.random.uniform(jax.random.fold_in(jax.random.fold_in(stream_key, 6), dim), (parts,), jnp.float32, least / len(split), largest / len(split))
        return jnp.repeat(jnp.exp(draws), extent[dim] // parts).reshape((-1,) + (1,) * (len(extent) - dim - 1))

    gain = one(*split[0])
    for cut in split[1:]:
        gain = gain * one(*cut)
    return gain


def gaussian(own_key, shape, width, bound, split=(), held_as=jnp.bfloat16):
    loudness = block_scale(own_key, shape, split, -0.22, 0.18) if split else 1.0
    values = jax.random.normal(own_key, shape, jnp.float32) * width * loudness
    return jnp.minimum(jnp.maximum(values, -bound), bound).astype(held_as)


def setup_inputs(seed: int = 0) -> dict:
    key_list = jax.random.split(jax.random.key(seed), 8)
    volume = gaussian(key_list[0], (CH, NX, NY, NZ), 1.0, 6.0, ((1, 16), (2, 4), (3, 4)), jnp.float32)
    forcing = gaussian(key_list[1], (CH, NX, NY, NZ), 1.0, 6.0, ((1, 16), (2, 4), (3, 4)), jnp.float32)
    medium = jnp.clip(0.5 + 2.5 * jax.random.uniform(key_list[2], (2, NX, NY, NZ), jnp.float32) ** block_scale(key_list[2], (2, NX, NY, NZ), ((1, 16), (2, 4), (3, 4)), -0.2, 0.2), 0.5, 3.0)
    points = jnp.clip(4.0 * jax.random.uniform(key_list[3], (3, POINTS), jnp.float32) ** block_scale(key_list[3], (3, POINTS), ((1, 256),), -0.2, 0.2), 0.0, 4.0)
    weights = jnp.clip(jnp.exp(math.log(0.5) - 2.3025851 * jax.random.uniform(key_list[4], (POINTS,), jnp.float32) ** block_scale(key_list[4], (POINTS,), ((0, 256),), -0.2, 0.2)), 0.05, 0.5)
    cell_map = plant(jax.random.randint(key_list[5], (POINTS,), 0, CX * CY * CZ), jax.random.fold_in(key_list[5], 1), 0, (CX * CY * CZ) - 1).astype(jnp.int32)
    near_list = draw_near_list(jax.random.fold_in(key_list[7], 71), 0)
    return dict(volume=volume, forcing=forcing, medium=medium, points=points, weights=weights, cell_map=cell_map, near_list=near_list)


FOUR_PI = 4.0 * 3.141592653589793
WAVENUMBER = 10.0
SOFTENING = 0.01
RELAX_RATE = 0.8
COUPLING = 0.5

def helmholtz(volume, medium):
    padded = jnp.pad(volume, ((0, 0), (1, 1), (1, 1), (1, 1)))
    beside = padded[:, 2:, 1:-1, 1:-1] + padded[:, :-2, 1:-1, 1:-1]
    beside = beside + padded[:, 1:-1, 2:, 1:-1] + padded[:, 1:-1, :-2, 1:-1]
    beside = beside + padded[:, 1:-1, 1:-1, 2:] + padded[:, 1:-1, 1:-1, :-2]
    laplace = 6.0 * volume - beside
    real_in = volume[:RHS]
    imag_in = volume[RHS:]
    real_out = laplace[:RHS] - medium[0] * real_in + medium[1] * imag_in
    imag_out = laplace[RHS:] - medium[0] * imag_in - medium[1] * real_in
    return jnp.concatenate([real_out, imag_out], 0)

def kernel_tiles(targets, sources, listed):
    delta_x = targets[0][:, None] - sources[0][None, :]
    delta_y = targets[1][:, None] - sources[1][None, :]
    delta_z = targets[2][:, None] - sources[2][None, :]
    distance = jnp.sqrt(delta_x * delta_x + delta_y * delta_y + delta_z * delta_z + SOFTENING)
    factor = listed / (FOUR_PI * distance)
    tile_real = (jnp.cos(WAVENUMBER * distance) * factor).astype(jnp.bfloat16)
    tile_imag = (jnp.sin(WAVENUMBER * distance) * factor).astype(jnp.bfloat16)
    return (tile_real, tile_imag)

def global_cells(cell_map):
    point_ids = jnp.arange(POINTS, dtype=jnp.int32)
    tile_ids = point_ids // B_DEV
    tile_x = tile_ids // (TY * TZ)
    tile_y = tile_ids // TZ % TY
    tile_z = tile_ids % TZ
    grid_x = tile_x * CX + cell_map // (CY * CZ)
    grid_y = tile_y * CY + cell_map // CZ % CY
    grid_z = tile_z * CZ + cell_map % CZ
    return ((grid_x * NY + grid_y) * NZ + grid_z).astype(jnp.int32)

def reference(volume, forcing, medium, points, weights, cell_map, near_list):
    residual = forcing - helmholtz(volume, medium)
    relaxed = volume + RELAX_RATE * residual / (6.0 - medium[0])[None]
    flat = relaxed.reshape(CH, NX * NY * NZ)
    cells = global_cells(cell_map)
    traces = (jnp.take(flat, cells, axis=1) * weights[None, :]).astype(jnp.bfloat16)
    contract = (((1,), (1,)), ((), ()))

    def one_cluster(number):
        targets = lax.dynamic_slice_in_dim(points, number * B_DEV, B_DEV, 1)
        near_row = lax.dynamic_index_in_dim(near_list, number, 0, keepdims=False)
        listed = jnp.repeat(near_row, B_DEV, total_repeat_length=POINTS).astype(jnp.float32)
        tile_real, tile_imag = kernel_tiles(targets, points, listed[None, :])
        real_sum = lax.dot_general(traces, tile_real, contract, preferred_element_type=jnp.float32)
        imag_sum = lax.dot_general(traces, tile_imag, contract, preferred_element_type=jnp.float32)
        return jnp.concatenate([real_sum[:RHS] - imag_sum[RHS:], real_sum[RHS:] + imag_sum[:RHS]], 0)
    blocks = lax.map(one_cluster, jnp.arange(TILES, dtype=jnp.int32))
    potential = jnp.transpose(blocks, (1, 0, 2)).reshape(CH, POINTS)
    spread = jnp.zeros((CH, NX * NY * NZ), jnp.float32).at[:, cells].add(potential)
    new_volume = relaxed + COUPLING * spread.reshape(relaxed.shape)
    return (new_volume, potential)
```

```python
import math

import jax
import jax.numpy as jnp
import numpy as np
from jax import lax
from jax.experimental import pallas as pl
from jax.experimental.pallas import tpu as pltpu
from jax.sharding import Mesh
from jax.sharding import PartitionSpec as P

RHS = 16
CX = 2
CY = 8
CZ = 128
CH = 32
PTS = 128

FOUR_PI = 4.0 * 3.141592653589793
WAVENUMBER = 10.0
SOFTENING = 0.01
RELAX_RATE = 0.8
COUPLING = 0.5

TURN = WAVENUMBER / (2.0 * 3.141592653589793)
CENTRE = 2.0
SCALE = TURN / FOUR_PI

ALPHA = ("zl", "core", "zh")
BETA = ("x", "y")
SIDE = 16
EXT = 32
NT = 4
LIST = 256 + 4 * NT

f32, bf16, i32 = jnp.float32, jnp.bfloat16, jnp.int32


def sine_coefficients():
    f = np.cos(np.linspace(0, np.pi / 2, 4001)) * 0.5 + 1e-9
    z = f * f
    y = np.sin(np.pi / 2 * f) / f
    basis = np.stack([np.ones_like(z), z, z * z], 1)
    weight = np.ones_like(f)
    fit = None
    for _ in range(300):
        fit, *_ = np.linalg.lstsq(basis * (weight * f)[:, None], y * weight * f, rcond=None)
        err = np.abs((basis @ fit - y) * f)
        weight = weight * (1e-12 + err / err.max()) ** 0.3
        weight = weight / weight.max()
    return [float(c) for c in fit]


SIN = sine_coefficients()
LAM2 = 2.0 * math.sqrt(2.0)
LAM = math.sqrt(LAM2)
RT2 = math.sqrt(2.0)
S0, S1, S2 = [c * LAM for c in SIN]


def dot(a, b, dims):
    return lax.dot_general(a, b, (dims, ((), ())), preferred_element_type=f32)


def split3(x):
    hi = x.astype(bf16).astype(f32)
    rest = x - hi
    mid = rest.astype(bf16).astype(f32)
    return hi, mid, rest - mid


def ext_kernel(where_ref, pts_ref, near_ref, src_ref, tgt_ref, flags_ref, scr):
    p = (pts_ref[...] - CENTRE) * TURN
    r = jnp.sum(p * p, axis=0, keepdims=True)
    ah, am, al = split3(-2.0 * p)
    bh, bm, bl = split3(p)
    sh, sm, sl = split3(r)
    th, tm, tl = split3(r + SOFTENING * TURN * TURN)
    one = jnp.ones((1, PTS), f32)
    for out, groups in (
        (src_ref, ((ah, sh), (ah, one), (am, sm), (am, one), (ah, sl), (al, one))),
        (tgt_ref, ((bh, one), (bm, th), (bh, one), (bm, tm), (bl, one), (bh, tl))),
    ):
        scr[...] = jnp.zeros((EXT, PTS), f32)
        for n, (three, last) in enumerate(groups):
            scr[4 * n : 4 * n + 3, :] = three
            scr[4 * n + 3 : 4 * n + 4, :] = last
        out[...] = scr[...].astype(bf16)
    base_row = where_ref[0]
    base_col = where_ref[1]
    rows = lax.broadcasted_iota(i32, (SIDE, 256), 0)
    cols = lax.broadcasted_iota(i32, (SIDE, 256), 1)
    pick_rows = (cols == rows * 4 + base_row).astype(f32).astype(bf16)
    rows = lax.broadcasted_iota(i32, (256, PTS), 0)
    cols = lax.broadcasted_iota(i32, (256, PTS), 1)
    pick_cols = ((rows == (cols // 4) * 64 + cols % 4 + base_col) & (cols < SIDE)).astype(f32).astype(bf16)
    near = (near_ref[...] != 0).astype(f32).astype(bf16)
    some = dot(pick_rows, near, ((1,), (0,))).astype(bf16)
    flags_ref[...] = dot(some, pick_cols, ((1,), (0,))).astype(i32)


def list_kernel(flags_ref, list_ref, count_ref):
    def clear(k, _):
        list_ref[k] = SIDE
        return 0

    lax.fori_loop(0, LIST, clear, 0)

    def one(k, n):
        i = k // SIDE
        j = k % SIDE
        list_ref[n] = jnp.where(flags_ref[i, j] != 0, i * 32 + j, SIDE)
        return n + flags_ref[i, j]

    count_ref[0] = lax.fori_loop(0, SIDE * SIDE, one, jnp.int32(0))


def faces_kernel(vol_ref, xu_ref, xd_ref, yu_ref, yd_ref, zu_ref, zd_ref):
    xu_ref[...] = vol_ref[:, CX - 1].astype(bf16)
    xd_ref[...] = vol_ref[:, 0].astype(bf16)
    yu_ref[...] = vol_ref[:, :, CY - 1, :].reshape(CH * CX, CZ).astype(bf16)
    yd_ref[...] = vol_ref[:, :, 0, :].reshape(CH * CX, CZ).astype(bf16)
    v = vol_ref[...].reshape(CH * CX * CY, CZ).astype(bf16)
    rows = lax.broadcasted_iota(i32, (16, CZ), 0)
    cols = lax.broadcasted_iota(i32, (16, CZ), 1)
    up = ((rows == 0) & (cols == CZ - 1)).astype(f32).astype(bf16)
    down = ((rows == 1) & (cols == 0)).astype(f32).astype(bf16)
    zu_ref[...] = dot(up, v, ((1,), (1,))).astype(bf16)
    zd_ref[...] = dot(down, v, ((1,), (1,))).astype(bf16)


def relax_kernel(vol_ref, forc_ref, med_ref, xl_ref, xh_ref, yl_ref, yh_ref, zl_ref, zh_ref,
                 wts_ref, map_ref, rel_ref, tr_ref):
    v = vol_ref[...]
    xl = xl_ref[...].astype(f32)
    xh = xh_ref[...].astype(f32)
    bx = jnp.stack([xl + v[:, 1], v[:, 0] + xh], axis=1)
    v3 = v.reshape(CH * CX, CY, CZ)
    row = lax.broadcasted_iota(i32, v3.shape, 1)
    yl = yl_ref[...].astype(f32)[:, None, :]
    yh = yh_ref[...].astype(f32)[:, None, :]
    by = jnp.where(row == 0, yl, pltpu.roll(v3, 1, 1)) + jnp.where(row == CY - 1, yh, pltpu.roll(v3, CY - 1, 1))
    v2 = v.reshape(CH * CX * CY, CZ)
    lane = lax.broadcasted_iota(i32, v2.shape, 1)
    rows = lax.broadcasted_iota(i32, (16, CZ), 0)
    cols = lax.broadcasted_iota(i32, (16, CZ), 1)
    place = (((rows == 0) & (cols == 0)) | ((rows == 1) & (cols == CZ - 1))).astype(f32).astype(bf16)
    zhalo = (zl_ref[...].astype(f32) + zh_ref[...].astype(f32)).astype(bf16)
    bz = (
        jnp.where(lane == 0, 0.0, pltpu.roll(v2, 1, 1))
        + jnp.where(lane == CZ - 1, 0.0, pltpu.roll(v2, CZ - 1, 1))
        + dot(zhalo, place, ((0,), (0,)))
    )
    beside = bx + by.reshape(v.shape) + bz.reshape(v.shape)
    a = med_ref[0]
    b = med_ref[1]
    lap = 6.0 * v - beside
    re, im = v[:RHS], v[RHS:]
    out_re = lap[:RHS] - a[None] * re + b[None] * im
    out_im = lap[RHS:] - a[None] * im - b[None] * re
    res = forc_ref[...] - jnp.concatenate([out_re, out_im], 0)
    rate = RELAX_RATE / (6.0 - a)
    relaxed = v + res * rate[None]
    rel_ref[...] = relaxed
    cells = map_ref[...]
    sub = lax.broadcasted_iota(i32, (CZ, PTS), 0)
    pick = (sub == cells % CZ).astype(f32).astype(bf16)
    hi, mid, lo = split3(relaxed.reshape(CH * CX * CY, CZ))
    at = (
        dot(hi.astype(bf16), pick, ((1,), (0,)))
        + dot(mid.astype(bf16), pick, ((1,), (0,)))
        + dot(lo.astype(bf16), pick, ((1,), (0,)))
    )
    rid = lax.broadcasted_iota(i32, (CX * CY, PTS), 0)
    keep = (rid == cells // CZ).astype(f32)
    at = at.reshape(CH, CX * CY, PTS) * keep[None]
    tr_ref[...] = (jnp.sum(at, axis=1) * wts_ref[...]).astype(bf16)


def evaluate(dist2):
    inv = lax.rsqrt(dist2)
    turns = dist2 * inv
    f = turns - jnp.round(turns)
    z = f * f
    s = f * ((S2 * z + S1) * z + S0)
    a = s * s
    c2 = RT2 - a
    w = LAM2 - a
    c = w * lax.rsqrt(w)
    s2 = s * c
    e = s2 * inv
    return (inv - e * s2).astype(bf16), (e * c2).astype(bf16)


def pair_kernel(list_ref, count_ref, src_ref, tgt_ref, tr_ref, out_ref, a_ref, w_ref, d0, d1, g0, g1):
    out_ref[...] = jnp.zeros_like(out_ref)
    for j in range(SIDE):
        a_ref[j] = jnp.transpose(src_ref[j].astype(f32)).astype(bf16)
        t = tr_ref[j]
        w_ref[j, :, 0:PTS] = t
        w_ref[j, :, PTS:] = jnp.concatenate([-t[RHS:], t[:RHS]], 0)
    a_ref[SIDE] = a_ref[0]
    w_ref[SIDE] = jnp.zeros((CH, 2 * PTS), bf16)
    pairs = (count_ref[0] + (2 * NT - 1)) // (2 * NT)

    def code(group, q):
        c = list_ref[group * NT + q]
        return c // 32, c % 32

    def dist(group, d_ref):
        for q in range(NT):
            i, j = code(group, q)
            d_ref[q] = jnp.dot(a_ref[j], tgt_ref[i], preferred_element_type=f32)

    def add(group, g_ref):
        for q in range(NT):
            i, j = code(group, q)
            out_ref[i] += jnp.dot(w_ref[j], g_ref[q], preferred_element_type=f32)

    def values(d_ref, g_ref):
        for q in range(NT):
            re, im = evaluate(d_ref[q])
            g_ref[q, 0:PTS, :] = re
            g_ref[q, PTS:, :] = im

    dist(0, d0)
    g1[...] = jnp.zeros_like(g1)

    def body(k, _):
        dist(2 * k + 1, d1)
        values(d0, g0)
        add(jnp.maximum(2 * k - 1, 0), g1)
        dist(2 * k + 2, d0)
        values(d1, g1)
        add(2 * k, g0)
        return 0

    lax.fori_loop(0, pairs, body, 0)
    add(jnp.maximum(2 * pairs - 1, 0), g1)


def finish_kernel(part_ref, rel_ref, map_ref, new_ref, pot_ref):
    pot = jnp.sum(part_ref[...].astype(f32), axis=0) * SCALE
    pot_ref[...] = pot
    cells = map_ref[...]
    rid = lax.broadcasted_iota(i32, (CX * CY, PTS), 0)
    keep = (rid == cells // CZ).astype(f32)
    sub = lax.broadcasted_iota(i32, (CZ, PTS), 0)
    pick = (sub == cells % CZ).astype(f32).astype(bf16)
    spread = jnp.zeros((CH * CX * CY, CZ), f32)
    for part in split3(pot * COUPLING):
        wide = (part[:, None, :] * keep[None]).reshape(CH * CX * CY, PTS).astype(bf16)
        spread = spread + dot(wide, pick, ((1,), (1,)))
    new_ref[...] = rel_ref[...] + spread.reshape(CH, CX, CY, CZ)


def vmem(n):
    return [pl.BlockSpec(memory_space=pltpu.VMEM)] * n


def smem(n):
    return [pl.BlockSpec(memory_space=pltpu.SMEM)] * n


def shaped(*shapes):
    return [jax.ShapeDtypeStruct(s, d) for s, d in shapes]


def step(x, axes, delta):
    size = 1
    for axis in axes:
        size *= lax.axis_size(axis)
    pairs = [(k, k + delta) for k in range(size) if 0 <= k + delta < size]
    return lax.ppermute(x, axes if len(axes) > 1 else axes[0], pairs)


def everyone(x, axes):
    return lax.all_to_all(jnp.broadcast_to(x[None], (SIDE,) + x.shape), axes, 0, 0, tiled=True)


def on_device(volume, forcing, medium, points, weights, cell_map, near_list):
    cells = cell_map[None, :]
    wts = weights[None, :]
    ax, ay = lax.axis_index("x"), lax.axis_index("y")
    alpha = lax.axis_index(ALPHA)
    where = jnp.stack([ax * 64 + ay, alpha * 4]).astype(i32)
    src, tgt, flags = pl.pallas_call(
        ext_kernel,
        out_shape=shaped(((EXT, PTS), bf16), ((EXT, PTS), bf16), ((SIDE, PTS), i32)),
        in_specs=smem(1) + vmem(2),
        out_specs=vmem(3),
        scratch_shapes=[pltpu.VMEM((EXT, PTS), f32)],
        name="ext",
    )(where, points, near_list)
    targets = everyone(tgt, ALPHA)
    sources = everyone(src, BETA)
    xu, xd, yu, yd, zu, zd = pl.pallas_call(
        faces_kernel,
        out_shape=shaped(
            *[((CH, CY, CZ), bf16)] * 2, *[((CH * CX, CZ), bf16)] * 2, *[((16, CH * CX * CY), bf16)] * 2
        ),
        in_specs=vmem(1),
        out_specs=vmem(6),
        name="faces",
    )(volume)
    grp = ("x", "zl", "core")
    xl, xh = step(xu, grp, 1), step(xd, grp, -1)
    yl, yh = step(yu, ("zh",), 1), step(yd, ("zh",), -1)
    zl, zh = step(zu, ("y",), 1), step(zd, ("y",), -1)
    order, count = pl.pallas_call(
        list_kernel,
        out_shape=shaped(((LIST,), i32), ((1,), i32)),
        in_specs=smem(1),
        out_specs=smem(2),
        name="order",
    )(flags)
    relaxed, traces = pl.pallas_call(
        relax_kernel,
        out_shape=shaped(((CH, CX, CY, CZ), f32), ((CH, PTS), bf16)),
        in_specs=vmem(11),
        out_specs=vmem(2),
        name="relax",
    )(volume, forcing, medium, xl, xh, yl, yh, zl, zh, wts, cells)
    source_traces = everyone(traces, BETA)
    part = pl.pallas_call(
        pair_kernel,
        out_shape=jax.ShapeDtypeStruct((SIDE, CH, PTS), f32),
        in_specs=smem(2) + vmem(3),
        out_specs=vmem(1)[0],
        scratch_shapes=[
            pltpu.VMEM((SIDE + 1, PTS, EXT), bf16),
            pltpu.VMEM((SIDE + 1, CH, 2 * PTS), bf16),
            pltpu.VMEM((NT, PTS, PTS), f32),
            pltpu.VMEM((NT, PTS, PTS), f32),
            pltpu.VMEM((NT, 2 * PTS, PTS), bf16),
            pltpu.VMEM((NT, 2 * PTS, PTS), bf16),
        ],
        name="pairs",
    )(order, count, sources, targets, source_traces)
    parts = lax.all_to_all(part, ALPHA, 0, 0, tiled=True)
    new_volume, potential = pl.pallas_call(
        finish_kernel,
        out_shape=shaped(((CH, CX, CY, CZ), f32), ((CH, PTS), f32)),
        in_specs=vmem(3),
        out_specs=vmem(2),
        name="finish",
    )(parts, relaxed, cells)
    return new_volume, potential


def solution(mesh):
    split = Mesh(np.asarray(mesh.devices).reshape(4, 2, 2, 4, 4), ("x", "zl", "core", "zh", "y"))
    grid = P(None, ("x", "zl", "core"), "zh", "y")
    all_axes = ("x", "zl", "core", "zh", "y")
    return jax.shard_map(
        on_device,
        mesh=split,
        in_specs=(grid, grid, grid, P(None, all_axes), P(all_axes), P(all_axes), P()),
        out_specs=(grid, P(None, all_axes)),
        check_vma=False,
    )
```

```python
import math

import jax
import jax.numpy as jnp
import numpy as np
from jax import lax
from jax.experimental import pallas as pl
from jax.experimental.pallas import tpu as pltpu
from jax.sharding import Mesh
from jax.sharding import PartitionSpec as P

RHS = 16
CX = 2
CY = 8
CZ = 128
CH = 32
PTS = 128

FOUR_PI = 4.0 * 3.141592653589793
WAVENUMBER = 10.0
SOFTENING = 0.01
RELAX_RATE = 0.8
COUPLING = 0.5

TURN = WAVENUMBER / (2.0 * 3.141592653589793)
CENTRE = 2.0
SCALE = TURN / FOUR_PI

AXES = ("x", "zl", "core", "zh", "y")
SIZES = dict(x=4, zl=2, core=2, zh=4, y=4)
STRIDES = dict(x=64, zl=32, core=16, zh=4, y=1)
ALPHA = ("x", "core", "y")
BETA = ("zl", "zh")
NA = math.prod(SIZES[a] for a in ALPHA)
NB = math.prod(SIZES[a] for a in BETA)
TILES = NA * NB
ROW = 64
EXT = 32
NT = 4
LIST = 384

f32, bf16, i32 = jnp.float32, jnp.bfloat16, jnp.int32


def sine_coefficients():
    f = np.cos(np.linspace(0, np.pi / 2, 4001)) * 0.5 + 1e-9
    z = f * f
    y = np.sin(np.pi / 2 * f) / f
    basis = np.stack([np.ones_like(z), z, z * z], 1)
    weight = np.ones_like(f)
    fit = None
    for _ in range(300):
        fit, *_ = np.linalg.lstsq(basis * (weight * f)[:, None], y * weight * f, rcond=None)
        err = np.abs((basis @ fit - y) * f)
        weight = weight * (1e-12 + err / err.max()) ** 0.3
        weight = weight / weight.max()
    return [float(c) for c in fit]


SIN = sine_coefficients()
LAM2 = 2.0 * math.sqrt(2.0)
LAM = math.sqrt(LAM2)
RT2 = math.sqrt(2.0)
S0, S1, S2 = [c * LAM for c in SIN]


def dot(a, b, dims):
    return lax.dot_general(a, b, (dims, ((), ())), preferred_element_type=f32)


def split3(x):
    hi = x.astype(bf16).astype(f32)
    rest = x - hi
    mid = rest.astype(bf16).astype(f32)
    return hi, mid, rest - mid


def cluster_of(index, axes):
    total = 0
    for axis in reversed(axes):
        total = total + (index % SIZES[axis]) * STRIDES[axis]
        index = index // SIZES[axis]
    return total


def own_part(axes):
    total = 0
    for axis in axes:
        total = total + lax.axis_index(axis) * STRIDES[axis]
    return total


def iota(shape, dim):
    return lax.broadcasted_iota(i32, shape, dim)


def mask(condition):
    return condition.astype(f32).astype(bf16)


def point_rows(pts, scr, src_ref, tgt_ref):
    p = (pts - CENTRE) * TURN
    r = jnp.sum(p * p, axis=0, keepdims=True)
    ah, am, al = split3(-2.0 * p)
    bh, bm, bl = split3(p)
    sh, sm, sl = split3(r)
    th, tm, tl = split3(r + SOFTENING * TURN * TURN)
    one = jnp.ones((1, PTS), f32)
    for out, groups in (
        (src_ref, ((ah, sh), (ah, one), (am, sm), (am, one), (ah, sl), (al, one))),
        (tgt_ref, ((bh, one), (bm, th), (bh, one), (bm, tm), (bl, one), (bh, tl))),
    ):
        scr[...] = jnp.zeros((EXT, PTS), f32)
        for n, (three, last) in enumerate(groups):
            scr[4 * n : 4 * n + 3, :] = three
            scr[4 * n + 3 : 4 * n + 4, :] = last
        rows = scr[...].astype(bf16)
        out[...] = jnp.broadcast_to(rows[None], out.shape) if len(out.shape) == 3 else rows


def tile_order(near, order_ref):
    pick_rows = mask(iota((NA, 256), 1) == cluster_of(iota((NA, 256), 0), ALPHA) + own_part(BETA))
    wide = iota((256, PTS), 1)
    pick_cols = mask((iota((256, PTS), 0) == cluster_of(wide, BETA) + own_part(ALPHA)) & (wide < NB))
    listed = dot(dot(pick_rows, near, ((1,), (0,))).astype(bf16), pick_cols, ((1,), (0,))).astype(bf16)
    k = iota((PTS, TILES), 1)
    flat = dot(listed, mask(iota((PTS, TILES), 0) == k % NB), ((1,), (0,)))
    own = iota((NA, TILES), 1) // NB == iota((NA, TILES), 0)
    flat = jnp.sum(jnp.where(own, flat, 0.0), axis=0, keepdims=True)
    square = (TILES, TILES)
    before = mask(iota(square, 0) < iota(square, 1))
    place = dot(jnp.broadcast_to(flat, (8, TILES)).astype(bf16), before, ((1,), (0,)))[0:1]
    hit = mask((place.astype(i32) == iota(square, 0)) & (flat > 0.5))
    k = iota((8, TILES), 1)
    row = iota((8, TILES), 0)
    codes = jnp.where(row == 0, k // NB, jnp.where(row == 1, k % NB, 0)).astype(f32).astype(bf16)
    found = dot(codes, hit, ((1,), (1,))).astype(i32)
    count = jnp.sum(flat, axis=1, keepdims=True).astype(i32)
    entry = jnp.where(iota((1, TILES), 1) < count, found[0:1] * ROW + found[1:2], NB)
    order_ref[...] = jnp.full((8, LIST), NB, i32)
    order_ref[0:1, 0:TILES] = entry
    order_ref[1:2, 0:PTS] = jnp.broadcast_to(count, (1, PTS))


def parities():
    return lax.axis_index("core") % 2, lax.axis_index("zh") % 2, lax.axis_index("y") % 2


def prep_kernel(vol_ref, pts_ref, near_ref, tgt_ref, src_ref, order_ref,
                xe_ref, xo_ref, ye_ref, yo_ref, ze_ref, zo_ref, scr):
    point_rows(pts_ref[...], scr, src_ref, tgt_ref)
    px, py, pz = parities()
    xe_ref[...] = vol_ref[:, 1 - px].astype(bf16)
    xo_ref[...] = vol_ref[:, px].astype(bf16)
    low = vol_ref[:, :, 0, :].reshape(CH * CX, CZ).astype(bf16)
    high = vol_ref[:, :, CY - 1, :].reshape(CH * CX, CZ).astype(bf16)
    ye_ref[...] = jnp.where(py == 0, high, low)
    yo_ref[...] = jnp.where(py == 0, low, high)
    v = vol_ref[...].reshape(CH * CX * CY, CZ).astype(bf16)
    row, col = iota((16, CZ), 0), iota((16, CZ), 1)
    up = mask((row == 0) & (col == CZ - 1))
    down = mask((row == 1) & (col == 0))
    ze_ref[...] = dot(jnp.where(pz == 0, up, down), v, ((1,), (1,))).astype(bf16)
    zo_ref[...] = dot(jnp.where(pz == 0, down, up), v, ((1,), (1,))).astype(bf16)
    tile_order(mask(near_ref[...] != 0), order_ref)


def relax_kernel(vol_ref, forc_ref, med_ref, xe_ref, xo_ref, ye_ref, yo_ref, ze_ref, zo_ref,
                 wts_ref, map_ref, src_ref, rel_ref, pack_ref):
    px, py, pz = parities()
    v = vol_ref[...]
    xe, xo = xe_ref[...].astype(f32), xo_ref[...].astype(f32)
    xl, xh = jnp.where(px == 0, xo, xe), jnp.where(px == 0, xe, xo)
    bx = jnp.stack([xl + v[:, 1], v[:, 0] + xh], axis=1)
    v3 = v.reshape(CH * CX, CY, CZ)
    row = iota(v3.shape, 1)
    ye, yo = ye_ref[...].astype(f32), yo_ref[...].astype(f32)
    yl, yh = jnp.where(py == 0, yo, ye)[:, None, :], jnp.where(py == 0, ye, yo)[:, None, :]
    by = jnp.where(row == 0, yl, pltpu.roll(v3, 1, 1)) + jnp.where(row == CY - 1, yh, pltpu.roll(v3, CY - 1, 1))
    v2 = v.reshape(CH * CX * CY, CZ)
    lane = iota(v2.shape, 1)
    row, col = iota((16, CZ), 0), iota((16, CZ), 1)
    place = mask(((row == 0) & (col == 0)) | ((row == 1) & (col == CZ - 1)))
    zhalo = (ze_ref[...].astype(f32) + zo_ref[...].astype(f32)).astype(bf16)
    bz = (
        jnp.where(lane == 0, 0.0, pltpu.roll(v2, 1, 1))
        + jnp.where(lane == CZ - 1, 0.0, pltpu.roll(v2, CZ - 1, 1))
        + dot(zhalo, place, ((0,), (0,)))
    )
    beside = bx + by.reshape(v.shape) + bz.reshape(v.shape)
    a = med_ref[0]
    b = med_ref[1]
    lap = 6.0 * v - beside
    re, im = v[:RHS], v[RHS:]
    out_re = lap[:RHS] - a[None] * re + b[None] * im
    out_im = lap[RHS:] - a[None] * im - b[None] * re
    res = forc_ref[...] - jnp.concatenate([out_re, out_im], 0)
    rate = RELAX_RATE / (6.0 - a)
    relaxed = v + res * rate[None]
    rel_ref[...] = relaxed
    cells = map_ref[...]
    pick = mask(iota((CZ, PTS), 0) == cells % CZ)
    hi, mid, lo = split3(relaxed.reshape(CH * CX * CY, CZ))
    at = (
        dot(hi.astype(bf16), pick, ((1,), (0,)))
        + dot(mid.astype(bf16), pick, ((1,), (0,)))
        + dot(lo.astype(bf16), pick, ((1,), (0,)))
    )
    keep = (iota((CX * CY, PTS), 0) == cells // CZ).astype(f32)
    at = at.reshape(CH, CX * CY, PTS) * keep[None]
    traces = (jnp.sum(at, axis=1) * wts_ref[...]).astype(bf16)
    pack_ref[:, 0:EXT, :] = jnp.broadcast_to(src_ref[...][None], (NB, EXT, PTS))
    pack_ref[:, EXT:, :] = jnp.broadcast_to(traces[None], (NB, CH, PTS))


def evaluate(dist2):
    inv = lax.rsqrt(dist2)
    turns = dist2 * inv
    f = turns - jnp.round(turns)
    z = f * f
    s = f * ((S2 * z + S1) * z + S0)
    a = s * s
    c2 = RT2 - a
    w = LAM2 - a
    c = w * lax.rsqrt(w)
    s2 = s * c
    e = s2 * inv
    return (inv - e * s2).astype(bf16), (e * c2).astype(bf16)


def pair_kernel(order_ref, pack_ref, tgt_ref, out_ref, a_ref, w_ref, d0, d1, g0, g1):
    out_ref[...] = jnp.zeros_like(out_ref)
    for j in range(NB):
        a_ref[j] = jnp.transpose(pack_ref[j, 0:EXT, :].astype(f32)).astype(bf16)
        t = pack_ref[j, EXT:, :]
        w_ref[j, :, 0:PTS] = t
        w_ref[j, :, PTS:] = jnp.concatenate([-t[RHS:], t[:RHS]], 0)
    a_ref[NB] = a_ref[0]
    w_ref[NB] = jnp.zeros((CH, 2 * PTS), bf16)
    pairs = (order_ref[1, 0] + (2 * NT - 1)) // (2 * NT)

    def code(group, q):
        c = order_ref[0, group * NT + q]
        return c // ROW, c % ROW

    def dist(group, d_ref):
        for q in range(NT):
            i, j = code(group, q)
            d_ref[q] = jnp.dot(a_ref[j], tgt_ref[i], preferred_element_type=f32)

    def add(group, g_ref):
        for q in range(NT):
            i, j = code(group, q)
            out_ref[i] += jnp.dot(w_ref[j], g_ref[q], preferred_element_type=f32)

    def values(d_ref, g_ref):
        for q in range(NT):
            re, im = evaluate(d_ref[q])
            g_ref[q, 0:PTS, :] = re
            g_ref[q, PTS:, :] = im

    dist(0, d0)
    g1[...] = jnp.zeros_like(g1)

    def body(k, _):
        dist(2 * k + 1, d1)
        values(d0, g0)
        add(jnp.maximum(2 * k - 1, 0), g1)
        dist(2 * k + 2, d0)
        values(d1, g1)
        add(2 * k, g0)
        return 0

    lax.fori_loop(0, pairs, body, 0)
    add(jnp.maximum(2 * pairs - 1, 0), g1)


def finish_kernel(part_ref, rel_ref, map_ref, new_ref, pot_ref):
    pot = jnp.sum(part_ref[...].astype(f32), axis=0) * SCALE
    pot_ref[...] = pot
    cells = map_ref[...]
    keep = (iota((CX * CY, PTS), 0) == cells // CZ).astype(f32)
    pick = mask(iota((CZ, PTS), 0) == cells % CZ)
    spread = jnp.zeros((CH * CX * CY, CZ), f32)
    for part in split3(pot * COUPLING):
        wide = (part[:, None, :] * keep[None]).reshape(CH * CX * CY, PTS).astype(bf16)
        spread = spread + dot(wide, pick, ((1,), (1,)))
    new_ref[...] = rel_ref[...] + spread.reshape(CH, CX, CY, CZ)


def call(kernel, name, args, spaces, outs, scratch=()):
    return pl.pallas_call(
        kernel,
        out_shape=[jax.ShapeDtypeStruct(shape, dtype) for shape, dtype in outs],
        in_specs=[pl.BlockSpec(memory_space=pltpu.SMEM if c == "s" else pltpu.VMEM) for c in spaces],
        out_specs=[pl.BlockSpec(memory_space=pltpu.VMEM)] * len(outs),
        scratch_shapes=[pltpu.VMEM(shape, dtype) for shape, dtype in scratch],
        name=name,
    )(*args)


def swap(x, axes, parity):
    size = math.prod(SIZES[a] for a in axes)
    pairs = [q for k in range(parity, size - 1, 2) for q in ((k, k + 1), (k + 1, k))]
    return lax.ppermute(x, axes if len(axes) > 1 else axes[0], pairs)


def on_device(volume, forcing, medium, points, weights, cell_map, near_list):
    cells = cell_map[None, :]
    face_x, face_y, face_z = (CH, CY, CZ), (CH * CX, CZ), (16, CH * CX * CY)
    tgt, src, order, xe, xo, ye, yo, ze, zo = call(
        prep_kernel,
        "prep",
        (volume, points, near_list),
        "vvv",
        [((NA, EXT, PTS), bf16), ((EXT, PTS), bf16), ((8, LIST), i32)]
        + [(face, bf16) for face in (face_x, face_x, face_y, face_y, face_z, face_z)],
        [((EXT, PTS), f32)],
    )
    targets = lax.all_to_all(tgt, ALPHA, 0, 0, tiled=True)
    grp = ("x", "zl", "core")
    ye, yo = swap(ye, ("zh",), 0), swap(yo, ("zh",), 1)
    ze, zo = swap(ze, ("y",), 0), swap(zo, ("y",), 1)
    xo, xe = swap(xo, grp, 1), swap(xe, grp, 0)
    relaxed, pack = call(
        relax_kernel,
        "relax",
        (volume, forcing, medium, xe, xo, ye, yo, ze, zo, weights[None, :], cells, src),
        "v" * 12,
        [((CH, CX, CY, CZ), f32), ((NB, EXT + CH, PTS), bf16)],
    )
    packs = lax.all_to_all(pack, BETA, 0, 0, tiled=True)
    (part,) = call(
        pair_kernel,
        "pairs",
        (order, packs, targets),
        "svv",
        [((NA, CH, PTS), f32)],
        [
            ((NB + 1, PTS, EXT), bf16),
            ((NB + 1, CH, 2 * PTS), bf16),
            ((NT, PTS, PTS), f32),
            ((NT, PTS, PTS), f32),
            ((NT, 2 * PTS, PTS), bf16),
            ((NT, 2 * PTS, PTS), bf16),
        ],
    )
    parts = lax.all_to_all(part, ALPHA, 0, 0, tiled=True)
    new_volume, potential = call(
        finish_kernel, "finish", (parts, relaxed, cells), "vvv", [((CH, CX, CY, CZ), f32), ((CH, PTS), f32)]
    )
    return new_volume, potential


def solution(mesh):
    split = Mesh(np.asarray(mesh.devices).reshape([SIZES[a] for a in AXES]), AXES)
    grid = P(None, ("x", "zl", "core"), "zh", "y")
    return jax.shard_map(
        on_device,
        mesh=split,
        in_specs=(grid, grid, grid, P(None, AXES), P(AXES), P(AXES), P()),
        out_specs=(grid, P(None, AXES)),
        check_vma=False,
    )
```

```python
import math

import jax
import jax.numpy as jnp
import numpy as np
from jax import lax
from jax.experimental import pallas as pl
from jax.experimental.pallas import tpu as pltpu
from jax.sharding import Mesh
from jax.sharding import PartitionSpec as P

RHS = 16
CX = 2
CY = 8
CZ = 128
CH = 32
PTS = 128

FOUR_PI = 4.0 * 3.141592653589793
WAVENUMBER = 10.0
SOFTENING = 0.01
RELAX_RATE = 0.8
COUPLING = 0.5

TURN = WAVENUMBER / (2.0 * 3.141592653589793)
CENTRE = 2.0
SCALE = TURN / FOUR_PI

AXES = ("x", "zl", "core", "zh", "y")
SIZES = dict(x=4, zl=2, core=2, zh=4, y=4)
STRIDES = dict(x=64, zl=32, core=16, zh=4, y=1)
ALPHA = ("x", "core", "y")
BETA = ("zl", "zh")
NA = math.prod(SIZES[a] for a in ALPHA)
NB = math.prod(SIZES[a] for a in BETA)
TILES = NA * NB
ROW = 64
EXT = 32
USED = 24
STRIPS = CH * CX * CY // CZ
NT = 4
LIST = 384

f32, bf16, i32 = jnp.float32, jnp.bfloat16, jnp.int32


def sine_coefficients():
    f = np.cos(np.linspace(0, np.pi / 2, 4001)) * 0.5 + 1e-9
    z = f * f
    y = np.sin(np.pi / 2 * f) / f
    basis = np.stack([np.ones_like(z), z, z * z], 1)
    weight = np.ones_like(f)
    fit = None
    for _ in range(300):
        fit, *_ = np.linalg.lstsq(basis * (weight * f)[:, None], y * weight * f, rcond=None)
        err = np.abs((basis @ fit - y) * f)
        weight = weight * (1e-12 + err / err.max()) ** 0.3
        weight = weight / weight.max()
    return [float(c) for c in fit]


SIN = sine_coefficients()
LAM2 = 2.0 * math.sqrt(2.0)
LAM = math.sqrt(LAM2)
RT2 = math.sqrt(2.0)
S0, S1, S2 = [c * LAM for c in SIN]


def dot(a, b, dims):
    return lax.dot_general(a, b, (dims, ((), ())), preferred_element_type=f32)


def split3(x):
    hi = x.astype(bf16).astype(f32)
    rest = x - hi
    mid = rest.astype(bf16).astype(f32)
    return hi, mid, rest - mid


def cluster_of(index, axes):
    total = 0
    for axis in reversed(axes):
        total = total + (index % SIZES[axis]) * STRIDES[axis]
        index = index // SIZES[axis]
    return total


def own_part(axes):
    total = 0
    for axis in axes:
        total = total + lax.axis_index(axis) * STRIDES[axis]
    return total


def iota(shape, dim):
    return lax.broadcasted_iota(i32, shape, dim)


def mask(condition):
    return condition.astype(f32).astype(bf16)


def point_rows(pts, ends, scr, src_ref, tgt_ref):
    p = (pts - CENTRE) * TURN
    r = jnp.sum(p * p, axis=0, keepdims=True)
    ah, am, al = split3(-2.0 * p)
    bh, bm, bl = split3(p)
    sh, sm, sl = split3(r)
    th, tm, tl = split3(r + SOFTENING * TURN * TURN)
    one = jnp.ones((1, PTS), f32)
    scr[...] = jnp.zeros((EXT, PTS), f32)

    def fill(*groups):
        for n, (three, last) in enumerate(groups):
            scr[4 * n : 4 * n + 3, :] = three
            scr[4 * n + 3 : 4 * n + 4, :] = last

    fill((ah, sh), (ah, one), (am, sm), (am, one), (ah, sl), (al, one))
    src_ref[...] = scr[...].astype(bf16)
    fill((bh, one), (bm, th), (bh, one), (bm, tm), (bl, one), (bh, tl))
    for k in range(STRIPS):
        for end in range(2):
            scr[USED + STRIPS * end + k : USED + STRIPS * end + k + 1, :] = ends[end : end + 1, CZ * k : CZ * (k + 1)]
    tgt_ref[...] = jnp.broadcast_to(scr[...].astype(bf16)[None], tgt_ref.shape)


def tile_order(near, order_ref):
    pick_rows = mask(iota((NA, 256), 1) == cluster_of(iota((NA, 256), 0), ALPHA) + own_part(BETA))
    wide = iota((256, PTS), 1)
    pick_cols = mask((iota((256, PTS), 0) == cluster_of(wide, BETA) + own_part(ALPHA)) & (wide < NB))
    listed = dot(dot(pick_rows, near, ((1,), (0,))).astype(bf16), pick_cols, ((1,), (0,))).astype(bf16)
    k = iota((PTS, TILES), 1)
    flat = dot(listed, mask(iota((PTS, TILES), 0) == k % NB), ((1,), (0,)))
    own = iota((NA, TILES), 1) // NB == iota((NA, TILES), 0)
    flat = jnp.sum(jnp.where(own, flat, 0.0), axis=0, keepdims=True)
    square = (TILES, TILES)
    before = mask(iota(square, 0) < iota(square, 1))
    place = dot(jnp.broadcast_to(flat, (8, TILES)).astype(bf16), before, ((1,), (0,)))[0:1]
    hit = mask((place.astype(i32) == iota(square, 0)) & (flat > 0.5))
    k = iota((8, TILES), 1)
    row = iota((8, TILES), 0)
    codes = jnp.where(row == 0, k // NB, jnp.where(row == 1, k % NB, 0)).astype(f32).astype(bf16)
    found = dot(codes, hit, ((1,), (1,))).astype(i32)
    count = jnp.sum(flat, axis=1, keepdims=True).astype(i32)
    entry = jnp.where(iota((1, TILES), 1) < count, found[0:1] * ROW + found[1:2], NB)
    order_ref[...] = jnp.full((8, LIST), NB, i32)
    order_ref[0:1, 0:TILES] = entry
    order_ref[1:2, 0:PTS] = jnp.broadcast_to(count, (1, PTS))


def parities():
    return lax.axis_index("core") % 2, lax.axis_index("zh") % 2


def prep_kernel(vol_ref, pts_ref, near_ref, tgt_ref, src_ref, order_ref, xe_ref, xo_ref, ye_ref, yo_ref, scr):
    v = vol_ref[...].reshape(CH * CX * CY, CZ).astype(bf16)
    row, col = iota((16, CZ), 0), iota((16, CZ), 1)
    pick = mask(((row == 0) & (col == CZ - 1)) | ((row == 1) & (col == 0)))
    point_rows(pts_ref[...], dot(pick, v, ((1,), (1,))), scr, src_ref, tgt_ref)
    px, py = parities()
    xe_ref[...] = vol_ref[:, 1 - px].astype(bf16)
    xo_ref[...] = vol_ref[:, px].astype(bf16)
    low = vol_ref[:, :, 0, :].reshape(CH * CX, CZ).astype(bf16)
    high = vol_ref[:, :, CY - 1, :].reshape(CH * CX, CZ).astype(bf16)
    ye_ref[...] = jnp.where(py == 0, high, low)
    yo_ref[...] = jnp.where(py == 0, low, high)
    tile_order(mask(near_ref[...] != 0), order_ref)


def joint_index(axes):
    total = 0
    for axis in axes:
        total = total * SIZES[axis] + lax.axis_index(axis)
    return total


def relax_kernel(vol_ref, forc_ref, med_ref, xe_ref, xo_ref, ye_ref, yo_ref, tgt_ref,
                 wts_ref, map_ref, src_ref, rel_ref, pack_ref, ends):
    px, py = parities()
    v = vol_ref[...]
    xe, xo = xe_ref[...].astype(f32), xo_ref[...].astype(f32)
    xl, xh = jnp.where(px == 0, xo, xe), jnp.where(px == 0, xe, xo)
    bx = jnp.stack([xl + v[:, 1], v[:, 0] + xh], axis=1)
    v3 = v.reshape(CH * CX, CY, CZ)
    row = iota(v3.shape, 1)
    ye, yo = ye_ref[...].astype(f32), yo_ref[...].astype(f32)
    yl, yh = jnp.where(py == 0, yo, ye)[:, None, :], jnp.where(py == 0, ye, yo)[:, None, :]
    by = jnp.where(row == 0, yl, pltpu.roll(v3, 1, 1)) + jnp.where(row == CY - 1, yh, pltpu.roll(v3, CY - 1, 1))
    v2 = v.reshape(CH * CX * CY, CZ)
    lane = iota(v2.shape, 1)
    row, col = iota((16, CZ), 0), iota((16, CZ), 1)
    place = mask(((row == 0) & (col == 0)) | ((row == 1) & (col == CZ - 1)))
    own, along = joint_index(ALPHA), lax.axis_index("y")
    half = EXT // 2
    before = tgt_ref[jnp.maximum(own - 1, 0), half:, :].astype(f32) * (along > 0).astype(f32)
    after = tgt_ref[jnp.minimum(own + 1, NA - 1), half:, :].astype(f32) * (along < SIZES["y"] - 1).astype(f32)
    ends[...] = jnp.zeros_like(ends)
    for k in range(STRIPS):
        spot = USED - half + k
        ends[0:1, CZ * k : CZ * (k + 1)] = before[spot : spot + 1]
        ends[1:2, CZ * k : CZ * (k + 1)] = after[spot + STRIPS : spot + STRIPS + 1]
    zhalo = ends[...].astype(bf16)
    bz = (
        jnp.where(lane == 0, 0.0, pltpu.roll(v2, 1, 1))
        + jnp.where(lane == CZ - 1, 0.0, pltpu.roll(v2, CZ - 1, 1))
        + dot(zhalo, place, ((0,), (0,)))
    )
    beside = bx + by.reshape(v.shape) + bz.reshape(v.shape)
    a = med_ref[0]
    b = med_ref[1]
    lap = 6.0 * v - beside
    re, im = v[:RHS], v[RHS:]
    out_re = lap[:RHS] - a[None] * re + b[None] * im
    out_im = lap[RHS:] - a[None] * im - b[None] * re
    res = forc_ref[...] - jnp.concatenate([out_re, out_im], 0)
    rate = RELAX_RATE / (6.0 - a)
    relaxed = v + res * rate[None]
    rel_ref[...] = relaxed
    cells = map_ref[...]
    pick = mask(iota((CZ, PTS), 0) == cells % CZ)
    hi, mid, lo = split3(relaxed.reshape(CH * CX * CY, CZ))
    at = (
        dot(hi.astype(bf16), pick, ((1,), (0,)))
        + dot(mid.astype(bf16), pick, ((1,), (0,)))
        + dot(lo.astype(bf16), pick, ((1,), (0,)))
    )
    keep = (iota((CX * CY, PTS), 0) == cells // CZ).astype(f32)
    at = at.reshape(CH, CX * CY, PTS) * keep[None]
    traces = (jnp.sum(at, axis=1) * wts_ref[...]).astype(bf16)
    pack_ref[:, 0:EXT, :] = jnp.broadcast_to(src_ref[...][None], (NB, EXT, PTS))
    pack_ref[:, EXT:, :] = jnp.broadcast_to(traces[None], (NB, CH, PTS))


def evaluate(dist2):
    inv = lax.rsqrt(dist2)
    turns = dist2 * inv
    f = turns - jnp.round(turns)
    z = f * f
    s = f * ((S2 * z + S1) * z + S0)
    a = s * s
    c2 = RT2 - a
    w = LAM2 - a
    c = w * lax.rsqrt(w)
    s2 = s * c
    over = SCALE * inv
    e = s2 * over
    return (over - e * s2).astype(bf16), (e * c2).astype(bf16)


def pair_kernel(order_ref, pack_ref, tgt_ref, out_ref, sum_ref, a_ref, w_ref, d0, d1, g0, g1):
    sum_ref[...] = jnp.zeros_like(sum_ref)
    for j in range(NB):
        a_ref[j] = jnp.transpose(pack_ref[j, 0:EXT, :].astype(f32)).astype(bf16)
        t = pack_ref[j, EXT:, :]
        w_ref[j, :, 0:PTS] = t
        w_ref[j, :, PTS:] = jnp.concatenate([-t[RHS:], t[:RHS]], 0)
    a_ref[NB] = a_ref[0]
    w_ref[NB] = jnp.zeros((CH, 2 * PTS), bf16)
    pairs = (order_ref[1, 0] + (2 * NT - 1)) // (2 * NT)

    def code(group, q):
        c = order_ref[0, group * NT + q]
        return c // ROW, c % ROW

    def dist(group, d_ref):
        for q in range(NT):
            i, j = code(group, q)
            d_ref[q] = jnp.dot(a_ref[j], tgt_ref[i], preferred_element_type=f32)

    def add(group, g_ref):
        for q in range(NT):
            i, j = code(group, q)
            sum_ref[i] += jnp.dot(w_ref[j], g_ref[q], preferred_element_type=f32)

    def values(d_ref, g_ref):
        for q in range(NT):
            re, im = evaluate(d_ref[q])
            g_ref[q, 0:PTS, :] = re
            g_ref[q, PTS:, :] = im

    dist(0, d0)
    g1[...] = jnp.zeros_like(g1)

    def body(k, _):
        dist(2 * k + 1, d1)
        values(d0, g0)
        add(jnp.maximum(2 * k - 1, 0), g1)
        dist(2 * k + 2, d0)
        values(d1, g1)
        add(2 * k, g0)
        return 0

    lax.fori_loop(0, pairs, body, 0)
    add(jnp.maximum(2 * pairs - 1, 0), g1)
    out_ref[...] = sum_ref[...].astype(bf16)


def finish_kernel(part_ref, rel_ref, map_ref, new_ref, pot_ref):
    pot = jnp.sum(part_ref[...].astype(f32), axis=0)
    pot_ref[...] = pot
    cells = map_ref[...]
    keep = (iota((CX * CY, PTS), 0) == cells // CZ).astype(f32)
    pick = mask(iota((CZ, PTS), 0) == cells % CZ)
    spread = jnp.zeros((CH * CX * CY, CZ), f32)
    for part in split3(pot * COUPLING):
        wide = (part[:, None, :] * keep[None]).reshape(CH * CX * CY, PTS).astype(bf16)
        spread = spread + dot(wide, pick, ((1,), (1,)))
    new_ref[...] = rel_ref[...] + spread.reshape(CH, CX, CY, CZ)


def call(kernel, name, args, spaces, outs, scratch=(), keep=True):
    args = [a if c == "s" else pltpu.with_memory_space_constraint(a, pltpu.VMEM) for a, c in zip(args, spaces)]
    shaped = pltpu.VMEM if keep else jax.ShapeDtypeStruct
    return pl.pallas_call(
        kernel,
        out_shape=[shaped(shape, dtype) for shape, dtype in outs],
        in_specs=[pl.BlockSpec(memory_space=pltpu.SMEM if c == "s" else pltpu.VMEM) for c in spaces],
        out_specs=[pl.BlockSpec(memory_space=pltpu.VMEM)] * len(outs),
        scratch_shapes=[pltpu.VMEM(shape, dtype) for shape, dtype in scratch],
        name=name,
    )(*args)


def swap(x, axes, parity):
    size = math.prod(SIZES[a] for a in axes)
    pairs = [q for k in range(parity, size - 1, 2) for q in ((k, k + 1), (k + 1, k))]
    return lax.ppermute(x, axes if len(axes) > 1 else axes[0], pairs)


def on_device(volume, forcing, medium, points, weights, cell_map, near_list):
    cells = cell_map[None, :]
    face_x, face_y = (CH, CY, CZ), (CH * CX, CZ)
    tgt, src, order, xe, xo, ye, yo = call(
        prep_kernel,
        "prep",
        (volume, points, near_list),
        "vvv",
        [((NA, EXT, PTS), bf16), ((EXT, PTS), bf16), ((8, LIST), i32)]
        + [(face, bf16) for face in (face_x, face_x, face_y, face_y)],
        [((EXT, PTS), f32)],
    )
    targets = lax.all_to_all(tgt, ALPHA, 0, 0, tiled=True)
    grp = ("x", "zl", "core")
    ye, yo = swap(ye, ("zh",), 0), swap(yo, ("zh",), 1)
    xo, xe = swap(xo, grp, 1), swap(xe, grp, 0)
    relaxed, pack = call(
        relax_kernel,
        "relax",
        (volume, forcing, medium, xe, xo, ye, yo, targets, weights[None, :], cells, src),
        "v" * 11,
        [((CH, CX, CY, CZ), f32), ((NB, EXT + CH, PTS), bf16)],
        [((16, CH * CX * CY), f32)],
    )
    packs = lax.all_to_all(pack, BETA, 0, 0, tiled=True)
    (part,) = call(
        pair_kernel,
        "pairs",
        (order, packs, targets),
        "svv",
        [((NA, CH, PTS), bf16)],
        [
            ((NA, CH, PTS), f32),
            ((NB + 1, PTS, EXT), bf16),
            ((NB + 1, CH, 2 * PTS), bf16),
            ((NT, PTS, PTS), f32),
            ((NT, PTS, PTS), f32),
            ((NT, 2 * PTS, PTS), bf16),
            ((NT, 2 * PTS, PTS), bf16),
        ],
    )
    parts = lax.all_to_all(part, ALPHA, 0, 0, tiled=True)
    new_volume, potential = call(
        finish_kernel,
        "finish",
        (parts, relaxed, cells),
        "vvv",
        [((CH, CX, CY, CZ), f32), ((CH, PTS), f32)],
        keep=False,
    )
    return new_volume, potential


def solution(mesh):
    split = Mesh(np.asarray(mesh.devices).reshape([SIZES[a] for a in AXES]), AXES)
    grid = P(None, ("x", "zl", "core"), "zh", "y")
    return jax.shard_map(
        on_device,
        mesh=split,
        in_specs=(grid, grid, grid, P(None, AXES), P(AXES), P(AXES), P()),
        out_specs=(grid, P(None, AXES)),
        check_vma=False,
    )
```

```python
import math

import jax
import jax.numpy as jnp
import numpy as np
from jax import lax
from jax.experimental import pallas as pl
from jax.experimental.pallas import tpu as pltpu
from jax.sharding import Mesh
from jax.sharding import PartitionSpec as P


RHS = 16
CX = 2
CY = 8
CZ = 128
CH = 32
PTS = 128

FOUR_PI = 4.0 * 3.141592653589793
WAVENUMBER = 10.0
SOFTENING = 0.01
RELAX_RATE = 0.8
COUPLING = 0.5

TURN = WAVENUMBER / (2.0 * 3.141592653589793)
CENTRE = 2.0
SCALE = TURN / FOUR_PI

AXES = ("x", "zl", "core", "zh", "y")
SIZES = dict(x=4, zl=2, core=2, zh=4, y=4)
STRIDES = dict(x=64, zl=32, core=16, zh=4, y=1)
ALPHA = ("x", "core", "y")
BETA = ("zl", "zh")
NA = math.prod(SIZES[a] for a in ALPHA)
NB = math.prod(SIZES[a] for a in BETA)
TILES = NA * NB
ROW = 64
EXT = 32
USED = 24
STRIPS = CH * CX * CY // CZ
NT = 4
LIST = 384

f32, bf16, i32 = jnp.float32, jnp.bfloat16, jnp.int32


def sine_coefficients():
    f = np.cos(np.linspace(0, np.pi / 2, 4001)) * 0.5 + 1e-9
    z = f * f
    y = np.sin(np.pi / 2 * f) / f
    basis = np.stack([np.ones_like(z), z, z * z], 1)
    weight = np.ones_like(f)
    fit = None
    for _ in range(300):
        fit, *_ = np.linalg.lstsq(basis * (weight * f)[:, None], y * weight * f, rcond=None)
        err = np.abs((basis @ fit - y) * f)
        weight = weight * (1e-12 + err / err.max()) ** 0.3
        weight = weight / weight.max()
    return [float(c) for c in fit]


SIN = sine_coefficients()
LAM2 = 2.0 * math.sqrt(2.0)
LAM = math.sqrt(LAM2)
RT2 = math.sqrt(2.0)
S0, S1, S2 = [c * LAM for c in SIN]


def dot(a, b, dims):
    return lax.dot_general(a, b, (dims, ((), ())), preferred_element_type=f32)


def split3(x):
    hi = x.astype(bf16).astype(f32)
    rest = x - hi
    mid = rest.astype(bf16).astype(f32)
    return hi, mid, rest - mid


def cluster_of(index, axes):
    total = 0
    for axis in reversed(axes):
        total = total + (index % SIZES[axis]) * STRIDES[axis]
        index = index // SIZES[axis]
    return total


def own_part(axes):
    total = 0
    for axis in axes:
        total = total + lax.axis_index(axis) * STRIDES[axis]
    return total


def iota(shape, dim):
    return lax.broadcasted_iota(i32, shape, dim)


def mask(condition):
    return condition.astype(f32).astype(bf16)


def point_rows(pts, ends, scr, src_ref, tgt_ref):
    p = (pts - CENTRE) * TURN
    r = jnp.sum(p * p, axis=0, keepdims=True)
    ah, am, al = split3(-2.0 * p)
    bh, bm, bl = split3(p)
    sh, sm, sl = split3(r)
    th, tm, tl = split3(r + SOFTENING * TURN * TURN)
    one = jnp.ones((1, PTS), f32)
    scr[...] = jnp.zeros((EXT, PTS), f32)

    def fill(*groups):
        for n, (three, last) in enumerate(groups):
            scr[4 * n : 4 * n + 3, :] = three
            scr[4 * n + 3 : 4 * n + 4, :] = last

    fill((ah, sh), (ah, one), (am, sm), (am, one), (ah, sl), (al, one))
    src_ref[...] = scr[...].astype(bf16)
    fill((bh, one), (bm, th), (bh, one), (bm, tm), (bl, one), (bh, tl))
    for k in range(STRIPS):
        for end in range(2):
            scr[USED + STRIPS * end + k : USED + STRIPS * end + k + 1, :] = ends[end : end + 1, CZ * k : CZ * (k + 1)]
    tgt_ref[...] = jnp.broadcast_to(scr[...].astype(bf16)[None], tgt_ref.shape)


def tile_order(near, order_ref):
    pick_rows = mask(iota((NA, 256), 1) == cluster_of(iota((NA, 256), 0), ALPHA) + own_part(BETA))
    wide = iota((256, PTS), 1)
    pick_cols = mask((iota((256, PTS), 0) == cluster_of(wide, BETA) + own_part(ALPHA)) & (wide < NB))
    listed = dot(dot(pick_rows, near, ((1,), (0,))).astype(bf16), pick_cols, ((1,), (0,))).astype(bf16)
    k = iota((PTS, TILES), 1)
    flat = dot(listed, mask(iota((PTS, TILES), 0) == k % NB), ((1,), (0,)))
    own = iota((NA, TILES), 1) // NB == iota((NA, TILES), 0)
    flat = jnp.sum(jnp.where(own, flat, 0.0), axis=0, keepdims=True)
    square = (TILES, TILES)
    before = mask(iota(square, 0) < iota(square, 1))
    place = dot(jnp.broadcast_to(flat, (8, TILES)).astype(bf16), before, ((1,), (0,)))[0:1]
    hit = mask((place.astype(i32) == iota(square, 0)) & (flat > 0.5))
    k = iota((8, TILES), 1)
    row = iota((8, TILES), 0)
    codes = jnp.where(row == 0, k // NB, jnp.where(row == 1, k % NB, 0)).astype(f32).astype(bf16)
    found = dot(codes, hit, ((1,), (1,))).astype(i32)
    count = jnp.sum(flat, axis=1, keepdims=True).astype(i32)
    entry = jnp.where(iota((1, TILES), 1) < count, found[0:1] * ROW + found[1:2], NB)
    order_ref[...] = jnp.full((8, LIST), NB, i32)
    order_ref[0:1, 0:TILES] = entry
    order_ref[1:2, 0:PTS] = jnp.broadcast_to(count, (1, PTS))


def parities():
    return lax.axis_index("core") % 2, lax.axis_index("zh") % 2


def prep_kernel(vol_ref, pts_ref, near_ref, wts_ref, map_ref, tgt_ref, src_ref, wts_out, map_out,
                xe_ref, xo_ref, ye_ref, yo_ref, order_ref, scr):
    wts_out[...] = wts_ref[...]
    map_out[...] = map_ref[...]
    v = vol_ref[...].reshape(CH * CX * CY, CZ).astype(bf16)
    row, col = iota((16, CZ), 0), iota((16, CZ), 1)
    pick = mask(((row == 0) & (col == CZ - 1)) | ((row == 1) & (col == 0)))
    point_rows(pts_ref[...], dot(pick, v, ((1,), (1,))), scr, src_ref, tgt_ref)
    px, py = parities()
    xe_ref[...] = vol_ref[:, 1 - px].astype(bf16)
    xo_ref[...] = vol_ref[:, px].astype(bf16)
    low = vol_ref[:, :, 0, :].reshape(CH * CX, CZ).astype(bf16)
    high = vol_ref[:, :, CY - 1, :].reshape(CH * CX, CZ).astype(bf16)
    ye_ref[...] = jnp.where(py == 0, high, low)
    yo_ref[...] = jnp.where(py == 0, low, high)
    tile_order(mask(near_ref[...] != 0), order_ref)


def joint_index(axes):
    total = 0
    for axis in axes:
        total = total * SIZES[axis] + lax.axis_index(axis)
    return total


def relax_kernel(vol_ref, forc_ref, med_ref, xe_ref, xo_ref, ye_ref, yo_ref, tgt_ref,
                 wts_ref, map_ref, src_ref, rel_ref, pack_ref, ends):
    px, py = parities()
    v = vol_ref[...]
    xe, xo = xe_ref[...].astype(f32), xo_ref[...].astype(f32)
    xl, xh = jnp.where(px == 0, xo, xe), jnp.where(px == 0, xe, xo)
    bx = jnp.stack([xl + v[:, 1], v[:, 0] + xh], axis=1)
    v3 = v.reshape(CH * CX, CY, CZ)
    row = iota(v3.shape, 1)
    ye, yo = ye_ref[...].astype(f32), yo_ref[...].astype(f32)
    yl, yh = jnp.where(py == 0, yo, ye)[:, None, :], jnp.where(py == 0, ye, yo)[:, None, :]
    by = jnp.where(row == 0, yl, pltpu.roll(v3, 1, 1)) + jnp.where(row == CY - 1, yh, pltpu.roll(v3, CY - 1, 1))
    v2 = v.reshape(CH * CX * CY, CZ)
    lane = iota(v2.shape, 1)
    row, col = iota((16, CZ), 0), iota((16, CZ), 1)
    place = mask(((row == 0) & (col == 0)) | ((row == 1) & (col == CZ - 1)))
    own, along = joint_index(ALPHA), lax.axis_index("y")
    half = EXT // 2
    before = tgt_ref[jnp.maximum(own - 1, 0), half:, :].astype(f32) * (along > 0).astype(f32)
    after = tgt_ref[jnp.minimum(own + 1, NA - 1), half:, :].astype(f32) * (along < SIZES["y"] - 1).astype(f32)
    ends[...] = jnp.zeros_like(ends)
    for k in range(STRIPS):
        spot = USED - half + k
        ends[0:1, CZ * k : CZ * (k + 1)] = before[spot : spot + 1]
        ends[1:2, CZ * k : CZ * (k + 1)] = after[spot + STRIPS : spot + STRIPS + 1]
    zhalo = ends[...].astype(bf16)
    bz = (
        jnp.where(lane == 0, 0.0, pltpu.roll(v2, 1, 1))
        + jnp.where(lane == CZ - 1, 0.0, pltpu.roll(v2, CZ - 1, 1))
        + dot(zhalo, place, ((0,), (0,)))
    )
    beside = bx + by.reshape(v.shape) + bz.reshape(v.shape)
    a = med_ref[0]
    b = med_ref[1]
    lap = 6.0 * v - beside
    re, im = v[:RHS], v[RHS:]
    out_re = lap[:RHS] - a[None] * re + b[None] * im
    out_im = lap[RHS:] - a[None] * im - b[None] * re
    res = forc_ref[...] - jnp.concatenate([out_re, out_im], 0)
    rate = RELAX_RATE / (6.0 - a)
    relaxed = v + res * rate[None]
    rel_ref[...] = relaxed
    cells = map_ref[...]
    pick = mask(iota((CZ, PTS), 0) == cells % CZ)
    hi, mid, lo = split3(relaxed.reshape(CH * CX * CY, CZ))
    at = (
        dot(hi.astype(bf16), pick, ((1,), (0,)))
        + dot(mid.astype(bf16), pick, ((1,), (0,)))
        + dot(lo.astype(bf16), pick, ((1,), (0,)))
    )
    keep = (iota((CX * CY, PTS), 0) == cells // CZ).astype(f32)
    at = at.reshape(CH, CX * CY, PTS) * keep[None]
    traces = (jnp.sum(at, axis=1) * wts_ref[...]).astype(bf16)
    pack_ref[:, 0:EXT, :] = jnp.broadcast_to(src_ref[...][None], (NB, EXT, PTS))
    pack_ref[:, EXT:, :] = jnp.broadcast_to(traces[None], (NB, CH, PTS))


def evaluate(dist2):
    inv = lax.rsqrt(dist2)
    turns = dist2 * inv
    f = turns - jnp.round(turns)
    z = f * f
    s = f * ((S2 * z + S1) * z + S0)
    a = s * s
    c2 = RT2 - a
    w = LAM2 - a
    c = w * lax.rsqrt(w)
    s2 = s * c
    over = SCALE * inv
    e = s2 * over
    return (over - e * s2).astype(bf16), (e * c2).astype(bf16)


def pair_kernel(order_ref, pack_ref, tgt_ref, out_ref, sum_ref, a_ref, w_ref, d0, d1, g0, g1):
    sum_ref[...] = jnp.zeros_like(sum_ref)
    for j in range(NB):
        a_ref[j] = jnp.transpose(pack_ref[j, 0:EXT, :].astype(f32)).astype(bf16)
        t = pack_ref[j, EXT:, :]
        w_ref[j, :, 0:PTS] = t
        w_ref[j, :, PTS:] = jnp.concatenate([-t[RHS:], t[:RHS]], 0)
    a_ref[NB] = a_ref[0]
    w_ref[NB] = jnp.zeros((CH, 2 * PTS), bf16)
    pairs = (order_ref[1, 0] + (2 * NT - 1)) // (2 * NT)

    def code(group, q):
        c = order_ref[0, group * NT + q]
        return c // ROW, c % ROW

    def dist(group, d_ref, q):
        i, j = code(group, q)
        d_ref[q] = jnp.dot(a_ref[j], tgt_ref[i], preferred_element_type=f32)

    def add(group, g_ref, q):
        i, j = code(group, q)
        sum_ref[i] += jnp.dot(w_ref[j], g_ref[q], preferred_element_type=f32)

    def values(d_ref, g_ref, q):
        re, im = evaluate(d_ref[q])
        g_ref[q, 0:PTS, :] = re
        g_ref[q, PTS:, :] = im

    for q in range(NT):
        dist(0, d0, q)
    g1[...] = jnp.zeros_like(g1)

    def body(k, _):
        for q in range(NT):
            dist(2 * k + 1, d1, q)
            values(d0, g0, q)
            add(jnp.maximum(2 * k - 1, 0), g1, q)
        for q in range(NT):
            dist(2 * k + 2, d0, q)
            values(d1, g1, q)
            add(2 * k, g0, q)
        return 0

    lax.fori_loop(0, pairs, body, 0)
    for q in range(NT):
        add(jnp.maximum(2 * pairs - 1, 0), g1, q)
    out_ref[...] = sum_ref[...].astype(bf16)


def finish_kernel(part_ref, rel_ref, map_ref, new_ref, pot_ref):
    pot = jnp.sum(part_ref[...].astype(f32), axis=0)
    pot_ref[...] = pot
    cells = map_ref[...]
    keep = (iota((CX * CY, PTS), 0) == cells // CZ).astype(f32)
    pick = mask(iota((CZ, PTS), 0) == cells % CZ)
    spread = jnp.zeros((CH * CX * CY, CZ), f32)
    for part in split3(pot * COUPLING):
        wide = (part[:, None, :] * keep[None]).reshape(CH * CX * CY, PTS).astype(bf16)
        spread = spread + dot(wide, pick, ((1,), (1,)))
    new_ref[...] = rel_ref[...] + spread.reshape(CH, CX, CY, CZ)


def call(kernel, args, spaces, outs, kept, scratch=()):
    args = [pltpu.with_memory_space_constraint(a, pltpu.VMEM) if c == "v" else a for a, c in zip(args, spaces)]
    return pl.pallas_call(
        kernel,
        out_shape=[
            (pltpu.VMEM if c == "v" else jax.ShapeDtypeStruct)(shape, dtype) for (shape, dtype), c in zip(outs, kept)
        ],
        in_specs=[pl.BlockSpec(memory_space=pltpu.SMEM if c == "s" else pltpu.VMEM) for c in spaces],
        out_specs=[pl.BlockSpec(memory_space=pltpu.VMEM)] * len(outs),
        scratch_shapes=[pltpu.VMEM(shape, dtype) for shape, dtype in scratch],
    )(*args)


def swap(x, axes, parity):
    size = math.prod(SIZES[a] for a in axes)
    pairs = [q for k in range(parity, size - 1, 2) for q in ((k, k + 1), (k + 1, k))]
    return lax.ppermute(x, axes if len(axes) > 1 else axes[0], pairs)


def sweep(volume, forcing, medium, points, weights, cell_map, near_list):
    face_x, face_y = (CH, CY, CZ), (CH * CX, CZ)
    tgt, src, wts, cells, xe, xo, ye, yo, order = call(
        prep_kernel,
        (volume, points, near_list, weights[None, :], cell_map[None, :]),
        "hhhhh",
        [((NA, EXT, PTS), bf16), ((EXT, PTS), bf16), ((1, PTS), f32), ((1, PTS), i32)]
        + [(face, bf16) for face in (face_x, face_x, face_y, face_y)]
        + [((8, LIST), i32)],
        "vvvvvvvvh",
        [((EXT, PTS), f32)],
    )
    grp = ("x", "zl", "core")
    ye = swap(ye, ("zh",), 0)
    yo = swap(yo, ("zh",), 1)
    xo = swap(xo, grp, 1)
    xe = swap(xe, grp, 0)
    targets = lax.all_to_all(tgt, ALPHA, 0, 0, tiled=True)
    relaxed, pack = call(
        relax_kernel,
        (volume, forcing, medium, xe, xo, ye, yo, targets, wts, cells, src),
        "v" * 11,
        [((CH, CX, CY, CZ), f32), ((NB, EXT + CH, PTS), bf16)],
        "vv",
        [((16, CH * CX * CY), f32)],
    )
    packs = lax.all_to_all(pack, BETA, 0, 0, tiled=True)
    (part,) = call(
        pair_kernel,
        (order, packs, targets),
        "svv",
        [((NA, CH, PTS), bf16)],
        "v",
        [
            ((NA, CH, PTS), f32),
            ((NB + 1, PTS, EXT), bf16),
            ((NB + 1, CH, 2 * PTS), bf16),
            ((NT, PTS, PTS), f32),
            ((NT, PTS, PTS), f32),
            ((NT, 2 * PTS, PTS), bf16),
            ((NT, 2 * PTS, PTS), bf16),
        ],
    )
    parts = lax.all_to_all(part, ALPHA, 0, 0, tiled=True)
    new_volume, potential = call(
        finish_kernel, (parts, relaxed, cells), "vvv", [((CH, CX, CY, CZ), f32), ((CH, PTS), f32)], "hh"
    )
    return new_volume, potential


def solution(mesh):
    split = Mesh(np.asarray(mesh.devices).reshape([SIZES[a] for a in AXES]), AXES)
    grid = P(None, ("x", "zl", "core"), "zh", "y")
    return jax.shard_map(
        sweep,
        mesh=split,
        in_specs=(grid, grid, grid, P(None, AXES), P(AXES), P(AXES), P()),
        out_specs=(grid, P(None, AXES)),
        check_vma=False,
    )
```

```python
import math

import jax
import jax.numpy as jnp
import numpy as np
from jax import lax
from jax.experimental import pallas as pl
from jax.experimental.pallas import tpu as pltpu
from jax.sharding import Mesh
from jax.sharding import PartitionSpec as P


RHS = 16
CX = 2
CY = 8
CZ = 128
CH = 32
PTS = 128

FOUR_PI = 4.0 * 3.141592653589793
WAVENUMBER = 10.0
SOFTENING = 0.01
RELAX_RATE = 0.8
COUPLING = 0.5

TURN = WAVENUMBER / (2.0 * 3.141592653589793)
CENTRE = 2.0
SCALE = TURN / FOUR_PI

AXES = ("x", "zl", "core", "zh", "y")
SIZES = dict(x=4, zl=2, core=2, zh=4, y=4)
STRIDES = dict(x=64, zl=32, core=16, zh=4, y=1)
ALPHA = ("x", "y")
BETA = ("zl", "core", "zh")
NA = math.prod(SIZES[a] for a in ALPHA)
NB = math.prod(SIZES[a] for a in BETA)
TILES = NA * NB
ROW = 64
EXT = 32
HALO = 16
BLOCK = 16
SOURCE_ROWS = (0, 1, 2, 9, 0, 1, 2, 12, 3, 4, 5, 10, 3, 4, 5, 12, 0, 1, 2, 11, 6, 7, 8, 12)
TARGET_ROWS = (0, 1, 2, 12, 3, 4, 5, 9, 0, 1, 2, 12, 3, 4, 5, 10, 6, 7, 8, 12, 0, 1, 2, 11)
NT = 4
LIST = 384

GRP = ("x", "zl", "core")
HALOS = tuple((f"halo_{n}{k}", axes) for n, axes in (("x", GRP), ("y", ("zh",)), ("z", ("y",))) for k in (0, 1))

f32, bf16, i32 = jnp.float32, jnp.bfloat16, jnp.int32


def sine_coefficients():
    f = np.cos(np.linspace(0, np.pi / 2, 4001)) * 0.5 + 1e-9
    z = f * f
    y = np.sin(np.pi / 2 * f) / f
    basis = np.stack([np.ones_like(z), z, z * z], 1)
    weight = np.ones_like(f)
    fit = None
    for _ in range(300):
        fit, *_ = np.linalg.lstsq(basis * (weight * f)[:, None], y * weight * f, rcond=None)
        err = np.abs((basis @ fit - y) * f)
        weight = weight * (1e-12 + err / err.max()) ** 0.3
        weight = weight / weight.max()
    return [float(c) for c in fit]


SIN = sine_coefficients()
LAM2 = 2.0 * math.sqrt(2.0)
LAM = math.sqrt(LAM2)
RT2 = math.sqrt(2.0)
S0, S1, S2 = [c * LAM for c in SIN]


def dot(a, b, dims):
    return lax.dot_general(a, b, (dims, ((), ())), preferred_element_type=f32)


def split3(x):
    hi = x.astype(bf16).astype(f32)
    rest = x - hi
    mid = rest.astype(bf16).astype(f32)
    return hi, mid, rest - mid


def cluster_of(index, axes):
    total = 0
    for axis in reversed(axes):
        total = total + (index % SIZES[axis]) * STRIDES[axis]
        index = index // SIZES[axis]
    return total


def own_part(axes):
    total = 0
    for axis in axes:
        total = total + lax.axis_index(axis) * STRIDES[axis]
    return total


def iota(shape, dim):
    return lax.broadcasted_iota(i32, shape, dim)


def mask(condition):
    return condition.astype(f32).astype(bf16)


def point_rows(pts, scr, src_ref, tgt_ref):
    p = (pts - CENTRE) * TURN
    r = jnp.sum(p * p, axis=0, keepdims=True)
    scr[...] = jnp.ones((BLOCK, PTS), f32)

    def fill(three, radius):
        for n, (part, single) in enumerate(zip(split3(three), split3(radius))):
            scr[3 * n : 3 * n + 3, :] = part
            scr[9 + n : 10 + n, :] = single

    fill(-2.0 * p, r)
    src_ref[...] = scr[...].astype(bf16)
    fill(p, r + SOFTENING * TURN * TURN)
    tgt_ref[...] = jnp.broadcast_to(scr[...].astype(bf16)[None], tgt_ref.shape)


def chooser(shape, along, rows):
    place, wanted = iota(shape, along), jnp.full(shape, -1, i32)
    for e, row in enumerate(rows):
        wanted = jnp.where(place == e, row, wanted)
    return mask(iota(shape, 1 - along) == wanted)


def tile_order(near, order_ref):
    pick_rows = mask(iota((NA, 256), 1) == cluster_of(iota((NA, 256), 0), ALPHA) + own_part(BETA))
    wide = iota((256, PTS), 1)
    pick_cols = mask((iota((256, PTS), 0) == cluster_of(wide, BETA) + own_part(ALPHA)) & (wide < NB))
    listed = dot(dot(pick_rows, near, ((1,), (0,))).astype(bf16), pick_cols, ((1,), (0,))).astype(bf16)
    k = iota((PTS, TILES), 1)
    flat = dot(listed, mask(iota((PTS, TILES), 0) == k % NB), ((1,), (0,)))
    own = iota((NA, TILES), 1) // NB == iota((NA, TILES), 0)
    flat = jnp.sum(jnp.where(own, flat, 0.0), axis=0, keepdims=True)
    square = (TILES, TILES)
    before = mask(iota(square, 0) < iota(square, 1))
    place = dot(jnp.broadcast_to(flat, (8, TILES)).astype(bf16), before, ((1,), (0,)))[0:1]
    hit = mask((place.astype(i32) == iota(square, 0)) & (flat > 0.5))
    k = iota((8, TILES), 1)
    row = iota((8, TILES), 0)
    codes = jnp.where(row == 0, k // NB, jnp.where(row == 1, k % NB, 0)).astype(f32).astype(bf16)
    found = dot(codes, hit, ((1,), (1,))).astype(i32)
    count = jnp.sum(flat, axis=1, keepdims=True).astype(i32)
    entry = jnp.where(iota((1, TILES), 1) < count, found[0:1] * ROW + found[1:2], NB)
    order_ref[...] = jnp.full((8, LIST), NB, i32)
    order_ref[0:1, 0:TILES] = entry
    order_ref[1:2, 0:PTS] = jnp.broadcast_to(count, (1, PTS))


def parities():
    return lax.axis_index("core") % 2, lax.axis_index("zh") % 2, lax.axis_index("y") % 2


def prep_kernel(vol_ref, pts_ref, near_ref, wts_ref, map_ref, tgt_ref, src_ref, wts_out, map_out,
                xe_ref, xo_ref, ye_ref, yo_ref, ze_ref, zo_ref, order_ref, scr):
    wts_out[...] = wts_ref[...]
    map_out[...] = map_ref[...]
    point_rows(pts_ref[...], scr, src_ref, tgt_ref)
    px, py, pz = parities()
    xe_ref[...] = vol_ref[:, 1 - px].astype(bf16)
    xo_ref[...] = vol_ref[:, px].astype(bf16)
    low = vol_ref[:, :, 0, :].reshape(CH * CX, CZ).astype(bf16)
    high = vol_ref[:, :, CY - 1, :].reshape(CH * CX, CZ).astype(bf16)
    ye_ref[...] = jnp.where(py == 0, high, low)
    yo_ref[...] = jnp.where(py == 0, low, high)
    v = vol_ref[...].reshape(CH * CX * CY, CZ).astype(bf16)
    row, col = iota((HALO, CZ), 0), iota((HALO, CZ), 1)
    up = mask((row == 0) & (col == CZ - 1))
    down = mask((row == 1) & (col == 0))
    ze_ref[...] = dot(jnp.where(pz == 0, up, down), v, ((1,), (1,))).astype(bf16)
    zo_ref[...] = dot(jnp.where(pz == 0, down, up), v, ((1,), (1,))).astype(bf16)
    tile_order(mask(near_ref[...] != 0), order_ref)


def relax_kernel(vol_ref, forc_ref, med_ref, xe_ref, xo_ref, ye_ref, yo_ref, ze_ref, zo_ref,
                 wts_ref, map_ref, src_ref, rel_ref, pack_ref):
    px, py, _ = parities()
    v = vol_ref[...]
    xe, xo = xe_ref[...].astype(f32), xo_ref[...].astype(f32)
    xl, xh = jnp.where(px == 0, xo, xe), jnp.where(px == 0, xe, xo)
    bx = jnp.stack([xl + v[:, 1], v[:, 0] + xh], axis=1)
    v3 = v.reshape(CH * CX, CY, CZ)
    row = iota(v3.shape, 1)
    ye, yo = ye_ref[...].astype(f32), yo_ref[...].astype(f32)
    yl, yh = jnp.where(py == 0, yo, ye)[:, None, :], jnp.where(py == 0, ye, yo)[:, None, :]
    by = jnp.where(row == 0, yl, pltpu.roll(v3, 1, 1)) + jnp.where(row == CY - 1, yh, pltpu.roll(v3, CY - 1, 1))
    v2 = v.reshape(CH * CX * CY, CZ)
    lane = iota(v2.shape, 1)
    row, col = iota((HALO, CZ), 0), iota((HALO, CZ), 1)
    place = mask(((row == 0) & (col == 0)) | ((row == 1) & (col == CZ - 1)))
    zhalo = (ze_ref[...].astype(f32) + zo_ref[...].astype(f32)).astype(bf16)
    bz = (
        jnp.where(lane == 0, 0.0, pltpu.roll(v2, 1, 1))
        + jnp.where(lane == CZ - 1, 0.0, pltpu.roll(v2, CZ - 1, 1))
        + dot(zhalo, place, ((0,), (0,)))
    )
    beside = bx + by.reshape(v.shape) + bz.reshape(v.shape)
    a = med_ref[0]
    b = med_ref[1]
    lap = 6.0 * v - beside
    re, im = v[:RHS], v[RHS:]
    out_re = lap[:RHS] - a[None] * re + b[None] * im
    out_im = lap[RHS:] - a[None] * im - b[None] * re
    res = forc_ref[...] - jnp.concatenate([out_re, out_im], 0)
    rate = RELAX_RATE / (6.0 - a)
    relaxed = v + res * rate[None]
    rel_ref[...] = relaxed
    cells = map_ref[...]
    pick = mask(iota((CZ, PTS), 0) == cells % CZ)
    hi, mid, lo = split3(relaxed.reshape(CH * CX * CY, CZ))
    at = (
        dot(hi.astype(bf16), pick, ((1,), (0,)))
        + dot(mid.astype(bf16), pick, ((1,), (0,)))
        + dot(lo.astype(bf16), pick, ((1,), (0,)))
    )
    keep = (iota((CX * CY, PTS), 0) == cells // CZ).astype(f32)
    at = at.reshape(CH, CX * CY, PTS) * keep[None]
    traces = (jnp.sum(at, axis=1) * wts_ref[...]).astype(bf16)
    pack_ref[:, 0:BLOCK, :] = jnp.broadcast_to(src_ref[...][None], (NB, BLOCK, PTS))
    pack_ref[:, BLOCK:, :] = jnp.broadcast_to(traces[None], (NB, CH, PTS))


def evaluate(dist2):
    inv = lax.rsqrt(dist2)
    turns = dist2 * inv
    f = turns - jnp.round(turns)
    z = f * f
    s = f * ((S2 * z + S1) * z + S0)
    a = s * s
    c2 = RT2 - a
    w = LAM2 - a
    c = w * lax.rsqrt(w)
    s2 = s * c
    over = SCALE * inv
    e = s2 * over
    return (over - e * s2).astype(bf16), (e * c2).astype(bf16)


def pair_kernel(order_ref, pack_ref, tgt_ref, out_ref, sum_ref, a_ref, b_ref, w_ref, d0, d1, g0, g1):
    sum_ref[...] = jnp.zeros_like(sum_ref)
    to_source = chooser((BLOCK, EXT), 1, SOURCE_ROWS)
    to_target = chooser((EXT, BLOCK), 0, TARGET_ROWS)
    for i in range(NA):
        b_ref[i] = dot(to_target, tgt_ref[i], ((1,), (0,))).astype(bf16)
    for j in range(NB):
        a_ref[j] = dot(pack_ref[j, 0:BLOCK, :], to_source, ((0,), (0,))).astype(bf16)
        t = pack_ref[j, BLOCK:, :]
        w_ref[j, :, 0:PTS] = t
        w_ref[j, :, PTS:] = jnp.concatenate([-t[RHS:], t[:RHS]], 0)
    a_ref[NB] = a_ref[0]
    w_ref[NB] = jnp.zeros((CH, 2 * PTS), bf16)
    pairs = (order_ref[1, 0] + (2 * NT - 1)) // (2 * NT)

    def code(group, q):
        c = order_ref[0, group * NT + q]
        return c // ROW, c % ROW

    def dist(group, d_ref, q):
        i, j = code(group, q)
        d_ref[q] = jnp.dot(a_ref[j], b_ref[i], preferred_element_type=f32)

    def add(group, g_ref, q):
        i, j = code(group, q)
        sum_ref[i] += jnp.dot(w_ref[j], g_ref[q], preferred_element_type=f32)

    def values(d_ref, g_ref, q):
        re, im = evaluate(d_ref[q])
        g_ref[q, 0:PTS, :] = re
        g_ref[q, PTS:, :] = im

    for q in range(NT):
        dist(0, d0, q)
    g1[...] = jnp.zeros_like(g1)

    def body(k, _):
        for q in range(NT):
            dist(2 * k + 1, d1, q)
            values(d0, g0, q)
            add(jnp.maximum(2 * k - 1, 0), g1, q)
        for q in range(NT):
            dist(2 * k + 2, d0, q)
            values(d1, g1, q)
            add(2 * k, g0, q)
        return 0

    lax.fori_loop(0, pairs, body, 0)
    for q in range(NT):
        add(jnp.maximum(2 * pairs - 1, 0), g1, q)
    out_ref[...] = sum_ref[...].astype(bf16)


def finish_kernel(part_ref, rel_ref, map_ref, new_ref, pot_ref):
    pot = jnp.sum(part_ref[...].astype(f32), axis=0)
    pot_ref[...] = pot
    cells = map_ref[...]
    keep = (iota((CX * CY, PTS), 0) == cells // CZ).astype(f32)
    pick = mask(iota((CZ, PTS), 0) == cells % CZ)
    spread = jnp.zeros((CH * CX * CY, CZ), f32)
    for part in split3(pot * COUPLING):
        wide = (part[:, None, :] * keep[None]).reshape(CH * CX * CY, PTS).astype(bf16)
        spread = spread + dot(wide, pick, ((1,), (1,)))
    new_ref[...] = rel_ref[...] + spread.reshape(CH, CX, CY, CZ)


def call(kernel, args, spaces, outs, kept, scratch=()):
    args = [pltpu.with_memory_space_constraint(a, pltpu.VMEM) if c == "v" else a for a, c in zip(args, spaces)]
    return pl.pallas_call(
        kernel,
        out_shape=[
            (pltpu.VMEM if c == "v" else jax.ShapeDtypeStruct)(shape, dtype) for (shape, dtype), c in zip(outs, kept)
        ],
        in_specs=[pl.BlockSpec(memory_space=pltpu.SMEM if c == "s" else pltpu.VMEM) for c in spaces],
        out_specs=[pl.BlockSpec(memory_space=pltpu.VMEM)] * len(outs),
        scratch_shapes=[pltpu.VMEM(shape, dtype) for shape, dtype in scratch],
    )(*args)


def swap(x, axes, parity):
    size = math.prod(SIZES[a] for a in axes)
    pairs = [q for k in range(parity, size - 1, 2) for q in ((k, k + 1), (k + 1, k))]
    return lax.ppermute(x, axes if len(axes) > 1 else axes[0], pairs)


def sweep(volume, forcing, medium, points, weights, cell_map, near_list):
    face_x, face_y, face_z = (CH, CY, CZ), (CH * CX, CZ), (HALO, CH * CX * CY)
    tgt, src, wts, cells, *faces, order = call(
        prep_kernel,
        (volume, points, near_list, weights[None, :], cell_map[None, :]),
        "hhhhh",
        [((NA, BLOCK, PTS), bf16), ((BLOCK, PTS), bf16), ((1, PTS), f32), ((1, PTS), i32)]
        + [(face, bf16) for face in (face_x, face_x, face_y, face_y, face_z, face_z)]
        + [((8, LIST), i32)],
        "v" * 10 + "h",
        [((BLOCK, PTS), f32)],
    )
    halos = []
    for face, (name, axes) in zip(faces, HALOS):
        halos.append(swap(face, axes, int(name[-1])))
    targets = lax.all_to_all(tgt, ALPHA, 0, 0, tiled=True)
    relaxed, pack = call(
        relax_kernel,
        (volume, forcing, medium, *halos, wts, cells, src),
        "v" * 12,
        [((CH, CX, CY, CZ), f32), ((NB, BLOCK + CH, PTS), bf16)],
        "vv",
    )
    packs = lax.all_to_all(pack, BETA, 0, 0, tiled=True)
    (part,) = call(
        pair_kernel,
        (order, packs, targets),
        "svv",
        [((NA, CH, PTS), bf16)],
        "v",
        [
            ((NA, CH, PTS), f32),
            ((NB + 1, PTS, EXT), bf16),
            ((NA, EXT, PTS), bf16),
            ((NB + 1, CH, 2 * PTS), bf16),
            ((NT, PTS, PTS), f32),
            ((NT, PTS, PTS), f32),
            ((NT, 2 * PTS, PTS), bf16),
            ((NT, 2 * PTS, PTS), bf16),
        ],
    )
    parts = lax.all_to_all(part, ALPHA, 0, 0, tiled=True)
    new_volume, potential = call(
        finish_kernel, (parts, relaxed, cells), "vvv", [((CH, CX, CY, CZ), f32), ((CH, PTS), f32)], "hh"
    )
    return new_volume, potential


def solution(mesh):
    split = Mesh(np.asarray(mesh.devices).reshape([SIZES[a] for a in AXES]), AXES)
    grid = P(None, ("x", "zl", "core"), "zh", "y")
    return jax.shard_map(
        sweep,
        mesh=split,
        in_specs=(grid, grid, grid, P(None, AXES), P(AXES), P(AXES), P()),
        out_specs=(grid, P(None, AXES)),
        check_vma=False,
    )
```

```python
import math

import jax
import jax.numpy as jnp
import numpy as np
from jax import lax
from jax.experimental import pallas as pl
from jax.experimental.pallas import tpu as pltpu
from jax.sharding import Mesh
from jax.sharding import PartitionSpec as P


RHS = 16
CX = 2
CY = 8
CZ = 128
CH = 32
PTS = 128

FOUR_PI = 4.0 * 3.141592653589793
WAVENUMBER = 10.0
SOFTENING = 0.01
RELAX_RATE = 0.8
COUPLING = 0.5

TURN = WAVENUMBER / (2.0 * 3.141592653589793)
CENTRE = 2.0
SCALE = TURN / FOUR_PI

AXES = ("x", "zl", "core", "zh", "y")
SIZES = dict(x=4, zl=2, core=2, zh=4, y=4)
STRIDES = dict(x=64, zl=32, core=16, zh=4, y=1)
ALPHA = ("core", "zh")
BETA = ("x", "zl", "y")
NA = math.prod(SIZES[a] for a in ALPHA)
NB = math.prod(SIZES[a] for a in BETA)
TILES = NA * NB
ROW = 64
EXT = 32
HALO = 16
FACE = CH * CY
SIDE = CH * CX
BLOCK = 16
SOURCE_ROWS = (0, 1, 2, 9, 0, 1, 2, 12, 3, 4, 5, 10, 3, 4, 5, 12, 0, 1, 2, 11, 6, 7, 8, 12)
TARGET_ROWS = (0, 1, 2, 12, 3, 4, 5, 9, 0, 1, 2, 12, 3, 4, 5, 10, 6, 7, 8, 12, 0, 1, 2, 11)
NT = 4
LIST = 384

GRP = ("x", "zl", "core")

f32, bf16, i32 = jnp.float32, jnp.bfloat16, jnp.int32


def sine_coefficients():
    f = np.cos(np.linspace(0, np.pi / 2, 4001)) * 0.5 + 1e-9
    z = f * f
    y = np.sin(np.pi / 2 * f) / f
    basis = np.stack([np.ones_like(z), z, z * z], 1)
    weight = np.ones_like(f)
    fit = None
    for _ in range(300):
        fit, *_ = np.linalg.lstsq(basis * (weight * f)[:, None], y * weight * f, rcond=None)
        err = np.abs((basis @ fit - y) * f)
        weight = weight * (1e-12 + err / err.max()) ** 0.3
        weight = weight / weight.max()
    return [float(c) for c in fit]


SIN = sine_coefficients()
LAM2 = 2.0 * math.sqrt(2.0)
LAM = math.sqrt(LAM2)
RT2 = math.sqrt(2.0)
S0, S1, S2 = [c * LAM for c in SIN]


def dot(a, b, dims):
    return lax.dot_general(a, b, (dims, ((), ())), preferred_element_type=f32)


def split3(x):
    hi = x.astype(bf16).astype(f32)
    rest = x - hi
    mid = rest.astype(bf16).astype(f32)
    return hi, mid, rest - mid


def cluster_of(index, axes):
    total = 0
    for axis in reversed(axes):
        total = total + (index % SIZES[axis]) * STRIDES[axis]
        index = index // SIZES[axis]
    return total


def own_part(axes):
    total = 0
    for axis in axes:
        total = total + lax.axis_index(axis) * STRIDES[axis]
    return total


def iota(shape, dim):
    return lax.broadcasted_iota(i32, shape, dim)


def mask(condition):
    return condition.astype(f32).astype(bf16)


def point_rows(pts, scr, src_ref, tgt_ref):
    p = (pts - CENTRE) * TURN
    r = jnp.sum(p * p, axis=0, keepdims=True)
    scr[...] = jnp.ones((BLOCK, PTS), f32)

    def fill(three, radius):
        for n, (part, single) in enumerate(zip(split3(three), split3(radius))):
            scr[3 * n : 3 * n + 3, :] = part
            scr[9 + n : 10 + n, :] = single

    fill(-2.0 * p, r)
    src_ref[...] = scr[...].astype(bf16)
    fill(p, r + SOFTENING * TURN * TURN)
    tgt_ref[...] = scr[...].astype(bf16)


def chooser(shape, along, rows):
    place, wanted = iota(shape, along), jnp.full(shape, -1, i32)
    for e, row in enumerate(rows):
        wanted = jnp.where(place == e, row, wanted)
    return mask(iota(shape, 1 - along) == wanted)


def target_place(slot):
    core, along = lax.axis_index("core"), lax.axis_index("zh")
    core = jnp.where(slot % 2 == 1, 1 - core, core)
    along = jnp.where(slot // 4 == 1, SIZES["zh"] - 1 - along, along)
    along = jnp.where((slot // 2) % 2 == 1, along + 1 - 2 * (along % 2), along)
    return core, along


def tile_order(near, order_ref):
    core, along = target_place(iota((NA, 256), 0))
    pick_rows = mask(iota((NA, 256), 1) == core * STRIDES["core"] + along * STRIDES["zh"] + own_part(BETA))
    wide = iota((256, PTS), 1)
    pick_cols = mask((iota((256, PTS), 0) == cluster_of(wide, BETA) + own_part(ALPHA)) & (wide < NB))
    listed = dot(dot(pick_rows, near, ((1,), (0,))).astype(bf16), pick_cols, ((1,), (0,))).astype(bf16)
    k = iota((PTS, TILES), 1)
    flat = dot(listed, mask(iota((PTS, TILES), 0) == k % NB), ((1,), (0,)))
    own = iota((NA, TILES), 1) // NB == iota((NA, TILES), 0)
    flat = jnp.sum(jnp.where(own, flat, 0.0), axis=0, keepdims=True)
    square = (TILES, TILES)
    before = mask(iota(square, 0) < iota(square, 1))
    place = dot(jnp.broadcast_to(flat, (8, TILES)).astype(bf16), before, ((1,), (0,)))[0:1]
    hit = mask((place.astype(i32) == iota(square, 0)) & (flat > 0.5))
    k = iota((8, TILES), 1)
    row = iota((8, TILES), 0)
    codes = jnp.where(row == 0, k // NB, jnp.where(row == 1, k % NB, 0)).astype(f32).astype(bf16)
    found = dot(codes, hit, ((1,), (1,))).astype(i32)
    count = jnp.sum(flat, axis=1, keepdims=True).astype(i32)
    entry = jnp.where(iota((1, TILES), 1) < count, found[0:1] * ROW + found[1:2], NB)
    order_ref[...] = jnp.full((8, LIST), NB, i32)
    order_ref[0:1, 0:TILES] = entry
    order_ref[1:2, 0:PTS] = jnp.broadcast_to(count, (1, PTS))


def parities():
    return lax.axis_index("core") % 2, lax.axis_index("zh") % 2, lax.axis_index("y") % 2


def prep_kernel(vol_ref, pts_ref, near_ref, wts_ref, map_ref, tgt_ref, src_ref, wts_out, map_out,
                xe_ref, xo_ref, ye_ref, yo_ref, ze_ref, zo_ref, order_ref, scr):
    wts_out[...] = wts_ref[...]
    map_out[...] = map_ref[...]
    point_rows(pts_ref[...], scr, src_ref, tgt_ref)
    px, py, pz = parities()
    xe_ref[0:FACE, :] = vol_ref[:, 1 - px].reshape(FACE, CZ).astype(bf16)
    xe_ref[FACE:, :] = tgt_ref[...]
    xo_ref[...] = vol_ref[:, px].reshape(FACE, CZ).astype(bf16)
    low = vol_ref[:, :, 0, :].reshape(CH * CX, CZ).astype(bf16)
    high = vol_ref[:, :, CY - 1, :].reshape(CH * CX, CZ).astype(bf16)
    ye_ref[...] = jnp.where(py == 0, high, low)
    yo_ref[...] = jnp.where(py == 0, low, high)
    v = vol_ref[...].reshape(CH * CX * CY, CZ).astype(bf16)
    row, col = iota((HALO, CZ), 0), iota((HALO, CZ), 1)
    up = mask((row == 0) & (col == CZ - 1))
    down = mask((row == 1) & (col == 0))
    ze_ref[...] = dot(jnp.where(pz == 0, up, down), v, ((1,), (1,))).astype(bf16)
    zo_ref[...] = dot(jnp.where(pz == 0, down, up), v, ((1,), (1,))).astype(bf16)
    tile_order(mask(near_ref[...] != 0), order_ref)


def near_kernel(face_ref, own_ref, core_ref, out_ref):
    out_ref[0:SIDE, :] = face_ref[...]
    out_ref[SIDE : SIDE + BLOCK, :] = own_ref[...]
    out_ref[SIDE + BLOCK :, :] = core_ref[FACE:, :]


def far_kernel(own_ref, core_ref, pair_ref, out_ref):
    out_ref[0:BLOCK, :] = own_ref[...]
    out_ref[BLOCK : 2 * BLOCK, :] = core_ref[FACE:, :]
    out_ref[2 * BLOCK :, :] = pair_ref[SIDE:, :]


def relax_kernel(vol_ref, forc_ref, med_ref, xe_ref, xo_ref, ye_ref, yo_ref, ze_ref, zo_ref,
                 wts_ref, map_ref, src_ref, rel_ref, pack_ref):
    px, py, _ = parities()
    v = vol_ref[...]
    xe = xe_ref[0:FACE, :].astype(f32).reshape(CH, CY, CZ)
    xo = xo_ref[...].astype(f32).reshape(CH, CY, CZ)
    xl, xh = jnp.where(px == 0, xo, xe), jnp.where(px == 0, xe, xo)
    bx = jnp.stack([xl + v[:, 1], v[:, 0] + xh], axis=1)
    v3 = v.reshape(CH * CX, CY, CZ)
    row = iota(v3.shape, 1)
    ye, yo = ye_ref[0:SIDE, :].astype(f32), yo_ref[...].astype(f32)
    yl, yh = jnp.where(py == 0, yo, ye)[:, None, :], jnp.where(py == 0, ye, yo)[:, None, :]
    by = jnp.where(row == 0, yl, pltpu.roll(v3, 1, 1)) + jnp.where(row == CY - 1, yh, pltpu.roll(v3, CY - 1, 1))
    v2 = v.reshape(CH * CX * CY, CZ)
    lane = iota(v2.shape, 1)
    row, col = iota((HALO, CZ), 0), iota((HALO, CZ), 1)
    place = mask(((row == 0) & (col == 0)) | ((row == 1) & (col == CZ - 1)))
    zhalo = (ze_ref[...].astype(f32) + zo_ref[...].astype(f32)).astype(bf16)
    bz = (
        jnp.where(lane == 0, 0.0, pltpu.roll(v2, 1, 1))
        + jnp.where(lane == CZ - 1, 0.0, pltpu.roll(v2, CZ - 1, 1))
        + dot(zhalo, place, ((0,), (0,)))
    )
    beside = bx + by.reshape(v.shape) + bz.reshape(v.shape)
    a = med_ref[0]
    b = med_ref[1]
    lap = 6.0 * v - beside
    re, im = v[:RHS], v[RHS:]
    out_re = lap[:RHS] - a[None] * re + b[None] * im
    out_im = lap[RHS:] - a[None] * im - b[None] * re
    res = forc_ref[...] - jnp.concatenate([out_re, out_im], 0)
    rate = RELAX_RATE / (6.0 - a)
    relaxed = v + res * rate[None]
    rel_ref[...] = relaxed
    cells = map_ref[...]
    pick = mask(iota((CZ, PTS), 0) == cells % CZ)
    hi, mid, lo = split3(relaxed.reshape(CH * CX * CY, CZ))
    at = (
        dot(hi.astype(bf16), pick, ((1,), (0,)))
        + dot(mid.astype(bf16), pick, ((1,), (0,)))
        + dot(lo.astype(bf16), pick, ((1,), (0,)))
    )
    keep = (iota((CX * CY, PTS), 0) == cells // CZ).astype(f32)
    at = at.reshape(CH, CX * CY, PTS) * keep[None]
    traces = (jnp.sum(at, axis=1) * wts_ref[...]).astype(bf16)
    pack_ref[:, 0:BLOCK, :] = jnp.broadcast_to(src_ref[...][None], (NB, BLOCK, PTS))
    pack_ref[:, BLOCK:, :] = jnp.broadcast_to(traces[None], (NB, CH, PTS))


def evaluate(dist2):
    inv = lax.rsqrt(dist2)
    turns = dist2 * inv
    f = turns - jnp.round(turns)
    z = f * f
    s = f * ((S2 * z + S1) * z + S0)
    a = s * s
    c2 = RT2 - a
    w = LAM2 - a
    c = w * lax.rsqrt(w)
    s2 = s * c
    over = SCALE * inv
    e = s2 * over
    return (over - e * s2).astype(bf16), (e * c2).astype(bf16)


def pair_kernel(order_ref, pack_ref, near_ref, far_ref, out_ref, sum_ref, a_ref, b_ref, w_ref, d0, d1, g0, g1):
    sum_ref[...] = jnp.zeros_like(sum_ref)
    to_source = chooser((BLOCK, EXT), 1, SOURCE_ROWS)
    to_target = chooser((EXT, BLOCK), 0, TARGET_ROWS)
    for i in range(NA):
        ref = near_ref if i < NA // 2 else far_ref
        start = i % (NA // 2) * BLOCK
        b_ref[i] = dot(to_target, ref[start : start + BLOCK, :], ((1,), (0,))).astype(bf16)
    for j in range(NB):
        a_ref[j] = dot(pack_ref[j, 0:BLOCK, :], to_source, ((0,), (0,))).astype(bf16)
        t = pack_ref[j, BLOCK:, :]
        w_ref[j, :, 0:PTS] = t
        w_ref[j, :, PTS:] = jnp.concatenate([-t[RHS:], t[:RHS]], 0)
    a_ref[NB] = a_ref[0]
    w_ref[NB] = jnp.zeros((CH, 2 * PTS), bf16)
    pairs = (order_ref[1, 0] + (2 * NT - 1)) // (2 * NT)

    def code(group, q):
        c = order_ref[0, group * NT + q]
        return c // ROW, c % ROW

    def dist(group, d_ref, q):
        i, j = code(group, q)
        d_ref[q] = jnp.dot(a_ref[j], b_ref[i], preferred_element_type=f32)

    def add(group, g_ref, q):
        i, j = code(group, q)
        sum_ref[i] += jnp.dot(w_ref[j], g_ref[q], preferred_element_type=f32)

    def values(d_ref, g_ref, q):
        re, im = evaluate(d_ref[q])
        g_ref[q, 0:PTS, :] = re
        g_ref[q, PTS:, :] = im

    for q in range(NT):
        dist(0, d0, q)
    g1[...] = jnp.zeros_like(g1)

    def body(k, _):
        for q in range(NT):
            dist(2 * k + 1, d1, q)
            values(d0, g0, q)
            add(jnp.maximum(2 * k - 1, 0), g1, q)
        for q in range(NT):
            dist(2 * k + 2, d0, q)
            values(d1, g1, q)
            add(2 * k, g0, q)
        return 0

    lax.fori_loop(0, pairs, body, 0)
    for q in range(NT):
        add(jnp.maximum(2 * pairs - 1, 0), g1, q)
    for i in range(NA):
        core, along = target_place(jnp.int32(i))
        out_ref[core * SIZES["zh"] + along] = sum_ref[i].astype(bf16)


def finish_kernel(part_ref, rel_ref, map_ref, new_ref, pot_ref):
    pot = jnp.sum(part_ref[...].astype(f32), axis=0)
    pot_ref[...] = pot
    cells = map_ref[...]
    keep = (iota((CX * CY, PTS), 0) == cells // CZ).astype(f32)
    pick = mask(iota((CZ, PTS), 0) == cells % CZ)
    spread = jnp.zeros((CH * CX * CY, CZ), f32)
    for part in split3(pot * COUPLING):
        wide = (part[:, None, :] * keep[None]).reshape(CH * CX * CY, PTS).astype(bf16)
        spread = spread + dot(wide, pick, ((1,), (1,)))
    new_ref[...] = rel_ref[...] + spread.reshape(CH, CX, CY, CZ)


def call(kernel, args, spaces, outs, kept, scratch=()):
    args = [pltpu.with_memory_space_constraint(a, pltpu.VMEM) if c == "v" else a for a, c in zip(args, spaces)]
    return pl.pallas_call(
        kernel,
        out_shape=[
            (pltpu.VMEM if c == "v" else jax.ShapeDtypeStruct)(shape, dtype) for (shape, dtype), c in zip(outs, kept)
        ],
        in_specs=[pl.BlockSpec(memory_space=pltpu.SMEM if c == "s" else pltpu.VMEM) for c in spaces],
        out_specs=[pl.BlockSpec(memory_space=pltpu.VMEM)] * len(outs),
        scratch_shapes=[pltpu.VMEM(shape, dtype) for shape, dtype in scratch],
    )(*args)


def swap(x, axes, parity):
    size = math.prod(SIZES[a] for a in axes)
    pairs = [q for k in range(parity, size - 1, 2) for q in ((k, k + 1), (k + 1, k))]
    return lax.ppermute(x, axes if len(axes) > 1 else axes[0], pairs)


def sweep(volume, forcing, medium, points, weights, cell_map, near_list):
    tgt, src, wts, cells, xe, xo, ye, yo, ze, zo, order = call(
        prep_kernel,
        (volume, points, near_list, weights[None, :], cell_map[None, :]),
        "hhhhh",
        [((BLOCK, PTS), bf16), ((BLOCK, PTS), bf16), ((1, PTS), f32), ((1, PTS), i32)]
        + [((rows, CZ), bf16) for rows in (FACE + BLOCK, FACE, SIDE, SIDE)]
        + [((HALO, CH * CX * CY), bf16)] * 2
        + [((8, LIST), i32)],
        "v" * 10 + "h",
        [((BLOCK, PTS), f32)],
    )
    xe = swap(xe, GRP, 0)
    xo = swap(xo, GRP, 1)
    yo = swap(yo, ("zh",), 1)
    ze = swap(ze, ("y",), 0)
    zo = swap(zo, ("y",), 1)
    (ye,) = call(near_kernel, (ye, tgt, xe), "vvv", [((SIDE + 2 * BLOCK, PTS), bf16)], "v")
    ye = swap(ye, ("zh",), 0)
    (quad,) = call(far_kernel, (tgt, xe, ye), "vvv", [((4 * BLOCK, PTS), bf16)], "v")
    mirror = [(k, SIZES["zh"] - 1 - k) for k in range(SIZES["zh"])]
    far = lax.ppermute(quad, "zh", mirror)
    relaxed, pack = call(
        relax_kernel,
        (volume, forcing, medium, xe, xo, ye, yo, ze, zo, wts, cells, src),
        "v" * 12,
        [((CH, CX, CY, CZ), f32), ((NB, BLOCK + CH, PTS), bf16)],
        "vv",
    )
    packs = lax.all_to_all(pack, BETA, 0, 0, tiled=True)
    (part,) = call(
        pair_kernel,
        (order, packs, quad, far),
        "svvv",
        [((NA, CH, PTS), bf16)],
        "v",
        [
            ((NA, CH, PTS), f32),
            ((NB + 1, PTS, EXT), bf16),
            ((NA, EXT, PTS), bf16),
            ((NB + 1, CH, 2 * PTS), bf16),
            ((NT, PTS, PTS), f32),
            ((NT, PTS, PTS), f32),
            ((NT, 2 * PTS, PTS), bf16),
            ((NT, 2 * PTS, PTS), bf16),
        ],
    )
    parts = lax.all_to_all(part, ALPHA, 0, 0, tiled=True)
    new_volume, potential = call(
        finish_kernel, (parts, relaxed, cells), "vvv", [((CH, CX, CY, CZ), f32), ((CH, PTS), f32)], "hh"
    )
    return new_volume, potential


def solution(mesh):
    split = Mesh(np.asarray(mesh.devices).reshape([SIZES[a] for a in AXES]), AXES)
    grid = P(None, ("x", "zl", "core"), "zh", "y")
    return jax.shard_map(
        sweep,
        mesh=split,
        in_specs=(grid, grid, grid, P(None, AXES), P(AXES), P(AXES), P()),
        out_specs=(grid, P(None, AXES)),
        check_vma=False,
    )
```

```python
import math

import jax
import jax.numpy as jnp
import numpy as np
from jax import lax
from jax.experimental import pallas as pl
from jax.experimental.pallas import tpu as pltpu
from jax.sharding import Mesh
from jax.sharding import PartitionSpec as P


RHS = 16
CX = 2
CY = 8
CZ = 128
CH = 32
PTS = 128

FOUR_PI = 4.0 * 3.141592653589793
WAVENUMBER = 10.0
SOFTENING = 0.01
RELAX_RATE = 0.8
COUPLING = 0.5

TURN = WAVENUMBER / (2.0 * 3.141592653589793)
CENTRE = 2.0
SCALE = TURN / FOUR_PI

AXES = ("x", "zl", "core", "zh", "y")
SIZES = dict(x=4, zl=2, core=2, zh=4, y=4)
STRIDES = dict(x=64, zl=32, core=16, zh=4, y=1)
ALPHA = ("core", "zh")
BETA = ("x", "zl", "y")
NA = math.prod(SIZES[a] for a in ALPHA)
NB = math.prod(SIZES[a] for a in BETA)
TILES = NA * NB
ROW = 64
EXT = 32
HALO = 16
FACE = CH * CY
SIDE = CH * CX
BLOCK = 16
SOURCE_ROWS = (0, 1, 2, 9, 0, 1, 2, 12, 3, 4, 5, 10, 3, 4, 5, 12, 0, 1, 2, 11, 6, 7, 8, 12)
TARGET_ROWS = (0, 1, 2, 12, 3, 4, 5, 9, 0, 1, 2, 12, 3, 4, 5, 10, 6, 7, 8, 12, 0, 1, 2, 11)
NT = 4
LIST = 384

GRP = ("x", "zl", "core")


f32, bf16, i32 = jnp.float32, jnp.bfloat16, jnp.int32


def sine_coefficients():
    f = np.cos(np.linspace(0, np.pi / 2, 4001)) * 0.5 + 1e-9
    z = f * f
    y = np.sin(np.pi / 2 * f) / f
    basis = np.stack([np.ones_like(z), z, z * z], 1)
    weight = np.ones_like(f)
    fit = None
    for _ in range(300):
        fit, *_ = np.linalg.lstsq(basis * (weight * f)[:, None], y * weight * f, rcond=None)
        err = np.abs((basis @ fit - y) * f)
        weight = weight * (1e-12 + err / err.max()) ** 0.3
        weight = weight / weight.max()
    return [float(c) for c in fit]


SIN = sine_coefficients()
LAM2 = 2.0 * math.sqrt(2.0)
LAM = math.sqrt(LAM2)
RT2 = math.sqrt(2.0)
S0, S1, S2 = [c * LAM for c in SIN]


def dot(a, b, dims):
    return lax.dot_general(a, b, (dims, ((), ())), preferred_element_type=f32)


def split3(x):
    hi = x.astype(bf16).astype(f32)
    rest = x - hi
    mid = rest.astype(bf16).astype(f32)
    return hi, mid, rest - mid


def cluster_of(index, axes):
    total = 0
    for axis in reversed(axes):
        total = total + (index % SIZES[axis]) * STRIDES[axis]
        index = index // SIZES[axis]
    return total


def own_part(axes):
    total = 0
    for axis in axes:
        total = total + lax.axis_index(axis) * STRIDES[axis]
    return total


def iota(shape, dim):
    return lax.broadcasted_iota(i32, shape, dim)


def mask(condition):
    return condition.astype(f32).astype(bf16)


def point_rows(pts, scr, src_ref, tgt_ref):
    p = (pts - CENTRE) * TURN
    r = jnp.sum(p * p, axis=0, keepdims=True)
    scr[...] = jnp.ones((BLOCK, PTS), f32)

    def fill(three, radius):
        for n, (part, single) in enumerate(zip(split3(three), split3(radius))):
            scr[3 * n : 3 * n + 3, :] = part
            scr[9 + n : 10 + n, :] = single

    fill(-2.0 * p, r)
    src_ref[...] = scr[...].astype(bf16)
    fill(p, r + SOFTENING * TURN * TURN)
    tgt_ref[...] = scr[...].astype(bf16)


def chooser(shape, along, rows):
    place, wanted = iota(shape, along), jnp.full(shape, -1, i32)
    for e, row in enumerate(rows):
        wanted = jnp.where(place == e, row, wanted)
    return mask(iota(shape, 1 - along) == wanted)


def target_place(slot):
    core, along = lax.axis_index("core"), lax.axis_index("zh")
    core = jnp.where(slot % 2 == 1, 1 - core, core)
    along = jnp.where(slot // 4 == 1, SIZES["zh"] - 1 - along, along)
    along = jnp.where((slot // 2) % 2 == 1, along + 1 - 2 * (along % 2), along)
    return core, along


def tile_order(near, order_ref):
    core, along = target_place(iota((NA, 256), 0))
    pick_rows = mask(iota((NA, 256), 1) == core * STRIDES["core"] + along * STRIDES["zh"] + own_part(BETA))
    wide = iota((256, PTS), 1)
    pick_cols = mask((iota((256, PTS), 0) == cluster_of(wide, BETA) + own_part(ALPHA)) & (wide < NB))
    listed = dot(dot(pick_rows, near, ((1,), (0,))).astype(bf16), pick_cols, ((1,), (0,))).astype(bf16)
    k = iota((PTS, TILES), 1)
    flat = dot(listed, mask(iota((PTS, TILES), 0) == k % NB), ((1,), (0,)))
    own = iota((NA, TILES), 1) // NB == iota((NA, TILES), 0)
    flat = jnp.sum(jnp.where(own, flat, 0.0), axis=0, keepdims=True)
    square = (TILES, TILES)
    before = mask(iota(square, 0) < iota(square, 1))
    place = dot(jnp.broadcast_to(flat, (8, TILES)).astype(bf16), before, ((1,), (0,)))[0:1]
    hit = mask((place.astype(i32) == iota(square, 0)) & (flat > 0.5))
    k = iota((8, TILES), 1)
    row = iota((8, TILES), 0)
    codes = jnp.where(row == 0, k // NB, jnp.where(row == 1, k % NB, 0)).astype(f32).astype(bf16)
    found = dot(codes, hit, ((1,), (1,))).astype(i32)
    count = jnp.sum(flat, axis=1, keepdims=True).astype(i32)
    entry = jnp.where(iota((1, TILES), 1) < count, found[0:1] * ROW + found[1:2], NB)
    order_ref[...] = jnp.full((8, LIST), NB, i32)
    order_ref[0:1, 0:TILES] = entry
    order_ref[1:2, 0:PTS] = jnp.broadcast_to(count, (1, PTS))


def parities():
    return lax.axis_index("core") % 2, lax.axis_index("zh") % 2, lax.axis_index("y") % 2


def order_kernel(near_ref, order_ref):
    tile_order(mask(near_ref[...] != 0), order_ref)


def prep_kernel(vol_ref, pts_ref, wts_ref, map_ref, tgt_ref, src_ref, vol_out, wts_out, map_out,
                xe_ref, xo_ref, ye_ref, yo_ref, ze_ref, zo_ref, scr):
    vol_out[...] = vol_ref[...]
    wts_out[...] = wts_ref[...]
    map_out[...] = map_ref[...]
    point_rows(pts_ref[...], scr, src_ref, tgt_ref)
    px, py, pz = parities()
    xe_ref[0:FACE, :] = vol_ref[:, 1 - px].reshape(FACE, CZ).astype(bf16)
    xe_ref[FACE:, :] = tgt_ref[...]
    xo_ref[...] = vol_ref[:, px].reshape(FACE, CZ).astype(bf16)
    low = vol_ref[:, :, 0, :].reshape(CH * CX, CZ).astype(bf16)
    high = vol_ref[:, :, CY - 1, :].reshape(CH * CX, CZ).astype(bf16)
    ye_ref[...] = jnp.where(py == 0, high, low)
    yo_ref[...] = jnp.where(py == 0, low, high)
    v = vol_ref[...].reshape(CH * CX * CY, CZ).astype(bf16)
    row, col = iota((HALO, CZ), 0), iota((HALO, CZ), 1)
    up = mask((row == 0) & (col == CZ - 1))
    down = mask((row == 1) & (col == 0))
    ze_ref[...] = dot(jnp.where(pz == 0, up, down), v, ((1,), (1,))).astype(bf16)
    zo_ref[...] = dot(jnp.where(pz == 0, down, up), v, ((1,), (1,))).astype(bf16)


def near_kernel(face_ref, own_ref, core_ref, out_ref):
    out_ref[0:SIDE, :] = face_ref[...]
    out_ref[SIDE : SIDE + BLOCK, :] = own_ref[...]
    out_ref[SIDE + BLOCK :, :] = core_ref[FACE:, :]


def far_kernel(own_ref, core_ref, pair_ref, out_ref):
    out_ref[0:BLOCK, :] = own_ref[...]
    out_ref[BLOCK : 2 * BLOCK, :] = core_ref[FACE:, :]
    out_ref[2 * BLOCK :, :] = pair_ref[SIDE:, :]


def relax_kernel(vol_ref, forc_ref, med_ref, xe_ref, xo_ref, ye_ref, yo_ref, ze_ref, zo_ref,
                 wts_ref, map_ref, src_ref, rel_ref, pack_ref):
    px, py, _ = parities()
    v = vol_ref[...]
    xe = xe_ref[0:FACE, :].astype(f32).reshape(CH, CY, CZ)
    xo = xo_ref[...].astype(f32).reshape(CH, CY, CZ)
    xl, xh = jnp.where(px == 0, xo, xe), jnp.where(px == 0, xe, xo)
    bx = jnp.stack([xl + v[:, 1], v[:, 0] + xh], axis=1)
    v3 = v.reshape(CH * CX, CY, CZ)
    row = iota(v3.shape, 1)
    ye, yo = ye_ref[0:SIDE, :].astype(f32), yo_ref[...].astype(f32)
    yl, yh = jnp.where(py == 0, yo, ye)[:, None, :], jnp.where(py == 0, ye, yo)[:, None, :]
    by = jnp.where(row == 0, yl, pltpu.roll(v3, 1, 1)) + jnp.where(row == CY - 1, yh, pltpu.roll(v3, CY - 1, 1))
    v2 = v.reshape(CH * CX * CY, CZ)
    lane = iota(v2.shape, 1)
    row, col = iota((HALO, CZ), 0), iota((HALO, CZ), 1)
    place = mask(((row == 0) & (col == 0)) | ((row == 1) & (col == CZ - 1)))
    zhalo = (ze_ref[...].astype(f32) + zo_ref[...].astype(f32)).astype(bf16)
    bz = (
        jnp.where(lane == 0, 0.0, pltpu.roll(v2, 1, 1))
        + jnp.where(lane == CZ - 1, 0.0, pltpu.roll(v2, CZ - 1, 1))
        + dot(zhalo, place, ((0,), (0,)))
    )
    beside = bx + by.reshape(v.shape) + bz.reshape(v.shape)
    a = med_ref[0]
    b = med_ref[1]
    lap = 6.0 * v - beside
    re, im = v[:RHS], v[RHS:]
    out_re = lap[:RHS] - a[None] * re + b[None] * im
    out_im = lap[RHS:] - a[None] * im - b[None] * re
    res = forc_ref[...] - jnp.concatenate([out_re, out_im], 0)
    rate = RELAX_RATE / (6.0 - a)
    relaxed = v + res * rate[None]
    rel_ref[...] = relaxed
    cells = map_ref[...]
    pick = mask(iota((CZ, PTS), 0) == cells % CZ)
    hi, mid, lo = split3(relaxed.reshape(CH * CX * CY, CZ))
    at = (
        dot(hi.astype(bf16), pick, ((1,), (0,)))
        + dot(mid.astype(bf16), pick, ((1,), (0,)))
        + dot(lo.astype(bf16), pick, ((1,), (0,)))
    )
    keep = (iota((CX * CY, PTS), 0) == cells // CZ).astype(f32)
    at = at.reshape(CH, CX * CY, PTS) * keep[None]
    traces = (jnp.sum(at, axis=1) * wts_ref[...]).astype(bf16)
    pack_ref[:, 0:BLOCK, :] = jnp.broadcast_to(src_ref[...][None], (NB, BLOCK, PTS))
    pack_ref[:, BLOCK:, :] = jnp.broadcast_to(traces[None], (NB, CH, PTS))


def evaluate(dist2):
    inv = lax.rsqrt(dist2)
    turns = dist2 * inv
    f = turns - jnp.round(turns)
    z = f * f
    s = f * ((S2 * z + S1) * z + S0)
    a = s * s
    c2 = RT2 - a
    w = LAM2 - a
    c = w * lax.rsqrt(w)
    s2 = s * c
    over = SCALE * inv
    e = s2 * over
    return (over - e * s2).astype(bf16), (e * c2).astype(bf16)


def pair_kernel(order_ref, pack_ref, near_ref, far_ref, out_ref, sum_ref, a_ref, b_ref, w_ref, d0, d1, g0, g1):
    sum_ref[...] = jnp.zeros_like(sum_ref)
    to_source = chooser((BLOCK, EXT), 1, SOURCE_ROWS)
    to_target = chooser((EXT, BLOCK), 0, TARGET_ROWS)
    for i in range(NA):
        ref = near_ref if i < NA // 2 else far_ref
        start = i % (NA // 2) * BLOCK
        b_ref[i] = dot(to_target, ref[start : start + BLOCK, :], ((1,), (0,))).astype(bf16)
    for j in range(NB):
        a_ref[j] = dot(pack_ref[j, 0:BLOCK, :], to_source, ((0,), (0,))).astype(bf16)
        t = pack_ref[j, BLOCK:, :]
        w_ref[j, :, 0:PTS] = t
        w_ref[j, :, PTS:] = jnp.concatenate([-t[RHS:], t[:RHS]], 0)
    a_ref[NB] = a_ref[0]
    w_ref[NB] = jnp.zeros((CH, 2 * PTS), bf16)
    pairs = (order_ref[1, 0] + (2 * NT - 1)) // (2 * NT)

    def code(group, q):
        c = order_ref[0, group * NT + q]
        return c // ROW, c % ROW

    def dist(group, d_ref, q):
        i, j = code(group, q)
        d_ref[q] = jnp.dot(a_ref[j], b_ref[i], preferred_element_type=f32)

    def add(group, g_ref, q):
        i, j = code(group, q)
        sum_ref[i] += jnp.dot(w_ref[j], g_ref[q], preferred_element_type=f32)

    def values(d_ref, g_ref, q):
        re, im = evaluate(d_ref[q])
        g_ref[q, 0:PTS, :] = re
        g_ref[q, PTS:, :] = im

    for q in range(NT):
        dist(0, d0, q)
    g1[...] = jnp.zeros_like(g1)

    def body(k, _):
        for q in range(NT):
            dist(2 * k + 1, d1, q)
            values(d0, g0, q)
            add(jnp.maximum(2 * k - 1, 0), g1, q)
        for q in range(NT):
            dist(2 * k + 2, d0, q)
            values(d1, g1, q)
            add(2 * k, g0, q)
        return 0

    lax.fori_loop(0, pairs, body, 0)
    for q in range(NT):
        add(jnp.maximum(2 * pairs - 1, 0), g1, q)
    for i in range(NA):
        core, along = target_place(jnp.int32(i))
        out_ref[core * SIZES["zh"] + along] = sum_ref[i].astype(bf16)


def finish_kernel(part_ref, rel_ref, map_ref, new_ref, pot_ref):
    pot = jnp.sum(part_ref[...].astype(f32), axis=0)
    pot_ref[...] = pot
    cells = map_ref[...]
    keep = (iota((CX * CY, PTS), 0) == cells // CZ).astype(f32)
    pick = mask(iota((CZ, PTS), 0) == cells % CZ)
    spread = jnp.zeros((CH * CX * CY, CZ), f32)
    for part in split3(pot * COUPLING):
        wide = (part[:, None, :] * keep[None]).reshape(CH * CX * CY, PTS).astype(bf16)
        spread = spread + dot(wide, pick, ((1,), (1,)))
    new_ref[...] = rel_ref[...] + spread.reshape(CH, CX, CY, CZ)


def call(kernel, args, spaces, outs, kept, scratch=()):
    args = [pltpu.with_memory_space_constraint(a, pltpu.VMEM) if c == "v" else a for a, c in zip(args, spaces)]
    return pl.pallas_call(
        kernel,
        out_shape=[
            (pltpu.VMEM if c == "v" else jax.ShapeDtypeStruct)(shape, dtype) for (shape, dtype), c in zip(outs, kept)
        ],
        in_specs=[pl.BlockSpec(memory_space=pltpu.SMEM if c == "s" else pltpu.VMEM) for c in spaces],
        out_specs=[pl.BlockSpec(memory_space=pltpu.VMEM)] * len(outs),
        scratch_shapes=[pltpu.VMEM(shape, dtype) for shape, dtype in scratch],
    )(*args)


def swap(x, axes, parity):
    size = math.prod(SIZES[a] for a in axes)
    pairs = [q for k in range(parity, size - 1, 2) for q in ((k, k + 1), (k + 1, k))]
    return lax.ppermute(x, axes if len(axes) > 1 else axes[0], pairs)


def sweep(volume, forcing, medium, points, weights, cell_map, near_list):
    tgt, src, vol, wts, cells, xe, xo, ye, yo, ze, zo = call(
        prep_kernel,
        (volume, points, weights[None, :], cell_map[None, :]),
        "hhhh",
        [((BLOCK, PTS), bf16), ((BLOCK, PTS), bf16), ((CH, CX, CY, CZ), f32), ((1, PTS), f32), ((1, PTS), i32)]
        + [((rows, CZ), bf16) for rows in (FACE + BLOCK, FACE, SIDE, SIDE)]
        + [((HALO, CH * CX * CY), bf16)] * 2,
        "v" * 11,
        [((BLOCK, PTS), f32)],
    )
    xe = swap(xe, GRP, 0)
    xo = swap(xo, GRP, 1)
    yo = swap(yo, ("zh",), 1)
    ze = swap(ze, ("y",), 0)
    zo = swap(zo, ("y",), 1)
    (ye,) = call(near_kernel, (ye, tgt, xe), "vvv", [((SIDE + 2 * BLOCK, PTS), bf16)], "v")
    ye = swap(ye, ("zh",), 0)
    (quad,) = call(far_kernel, (tgt, xe, ye), "vvv", [((4 * BLOCK, PTS), bf16)], "v")
    mirror = [(k, SIZES["zh"] - 1 - k) for k in range(SIZES["zh"])]
    far = lax.ppermute(quad, "zh", mirror)
    relaxed, pack = call(
        relax_kernel,
        (vol, forcing, medium, xe, xo, ye, yo, ze, zo, wts, cells, src),
        "v" * 12,
        [((CH, CX, CY, CZ), f32), ((NB, BLOCK + CH, PTS), bf16)],
        "vv",
    )
    packs = lax.all_to_all(pack, BETA, 0, 0, tiled=True)
    (order,) = call(order_kernel, (near_list,), "v", [((8, LIST), i32)], "h")
    (part,) = call(
        pair_kernel,
        (order, packs, quad, far),
        "svvv",
        [((NA, CH, PTS), bf16)],
        "v",
        [
            ((NA, CH, PTS), f32),
            ((NB + 1, PTS, EXT), bf16),
            ((NA, EXT, PTS), bf16),
            ((NB + 1, CH, 2 * PTS), bf16),
            ((NT, PTS, PTS), f32),
            ((NT, PTS, PTS), f32),
            ((NT, 2 * PTS, PTS), bf16),
            ((NT, 2 * PTS, PTS), bf16),
        ],
    )
    parts = lax.all_to_all(part, ALPHA, 0, 0, tiled=True)
    new_volume, potential = call(
        finish_kernel, (parts, relaxed, cells), "vvv", [((CH, CX, CY, CZ), f32), ((CH, PTS), f32)], "hh"
    )
    return new_volume, potential


def solution(mesh):
    split = Mesh(np.asarray(mesh.devices).reshape([SIZES[a] for a in AXES]), AXES)
    grid = P(None, ("x", "zl", "core"), "zh", "y")
    return jax.shard_map(
        sweep,
        mesh=split,
        in_specs=(grid, grid, grid, P(None, AXES), P(AXES), P(AXES), P()),
        out_specs=(grid, P(None, AXES)),
        check_vma=False,
    )
```

```python
import math

import jax
import jax.numpy as jnp
import numpy as np
from jax import lax
from jax.experimental import pallas as pl
from jax.experimental.pallas import tpu as pltpu
from jax.sharding import Mesh
from jax.sharding import PartitionSpec as P


RHS = 16
CX = 2
CY = 8
CZ = 128
CH = 32
PTS = 128

FOUR_PI = 4.0 * 3.141592653589793
WAVENUMBER = 10.0
SOFTENING = 0.01
RELAX_RATE = 0.8
COUPLING = 0.5

TURN = WAVENUMBER / (2.0 * 3.141592653589793)
CENTRE = 2.0
SCALE = TURN / FOUR_PI

AXES = ("x", "zl", "core", "zh", "y")
SIZES = dict(x=4, zl=2, core=2, zh=4, y=4)
STRIDES = dict(x=64, zl=32, core=16, zh=4, y=1)
ALPHA = ("core", "zh")
BETA = ("x", "zl", "y")
NA = math.prod(SIZES[a] for a in ALPHA)
NB = math.prod(SIZES[a] for a in BETA)
TILES = NA * NB
ROW = 64
EXT = 32
HALO = 16
FACE = CH * CY
SIDE = CH * CX
BLOCK = 16
SOURCE_ROWS = (0, 1, 2, 9, 0, 1, 2, 12, 3, 4, 5, 10, 3, 4, 5, 12, 0, 1, 2, 11, 6, 7, 8, 12)
TARGET_ROWS = (0, 1, 2, 12, 3, 4, 5, 9, 0, 1, 2, 12, 3, 4, 5, 10, 6, 7, 8, 12, 0, 1, 2, 11)
NT = 4
LIST = 384

GRP = ("x", "zl", "core")


f32, bf16, i32 = jnp.float32, jnp.bfloat16, jnp.int32


def sine_coefficients():
    f = np.cos(np.linspace(0, np.pi / 2, 4001)) * 0.5 + 1e-9
    z = f * f
    y = np.sin(np.pi / 2 * f) / f
    basis = np.stack([np.ones_like(z), z, z * z], 1)
    weight = np.ones_like(f)
    fit = None
    for _ in range(300):
        fit, *_ = np.linalg.lstsq(basis * (weight * f)[:, None], y * weight * f, rcond=None)
        err = np.abs((basis @ fit - y) * f)
        weight = weight * (1e-12 + err / err.max()) ** 0.3
        weight = weight / weight.max()
    return [float(c) for c in fit]


SIN = sine_coefficients()
LAM2 = 2.0 * math.sqrt(2.0)
LAM = math.sqrt(LAM2)
RT2 = math.sqrt(2.0)
S0, S1, S2 = [c * LAM for c in SIN]


def dot(a, b, dims):
    return lax.dot_general(a, b, (dims, ((), ())), preferred_element_type=f32)


def split3(x):
    hi = x.astype(bf16).astype(f32)
    rest = x - hi
    mid = rest.astype(bf16).astype(f32)
    return hi, mid, rest - mid


def cluster_of(index, axes):
    total = 0
    for axis in reversed(axes):
        total = total + (index % SIZES[axis]) * STRIDES[axis]
        index = index // SIZES[axis]
    return total


def own_part(axes):
    total = 0
    for axis in axes:
        total = total + lax.axis_index(axis) * STRIDES[axis]
    return total


def iota(shape, dim):
    return lax.broadcasted_iota(i32, shape, dim)


def mask(condition):
    return condition.astype(f32).astype(bf16)


def point_rows(pts, scr, src_ref, tgt_ref):
    p = (pts - CENTRE) * TURN
    r = jnp.sum(p * p, axis=0, keepdims=True)
    scr[...] = jnp.ones((BLOCK, PTS), f32)

    def fill(three, radius):
        for n, (part, single) in enumerate(zip(split3(three), split3(radius))):
            scr[3 * n : 3 * n + 3, :] = part
            scr[9 + n : 10 + n, :] = single

    fill(-2.0 * p, r)
    src_ref[...] = scr[...].astype(bf16)
    fill(p, r + SOFTENING * TURN * TURN)
    tgt_ref[...] = scr[...].astype(bf16)


def chooser(shape, along, rows):
    place, wanted = iota(shape, along), jnp.full(shape, -1, i32)
    for e, row in enumerate(rows):
        wanted = jnp.where(place == e, row, wanted)
    return mask(iota(shape, 1 - along) == wanted)


def target_place(slot):
    core, along = lax.axis_index("core"), lax.axis_index("zh")
    core = jnp.where(slot % 2 == 1, 1 - core, core)
    along = jnp.where(slot // 4 == 1, SIZES["zh"] - 1 - along, along)
    along = jnp.where((slot // 2) % 2 == 1, along + 1 - 2 * (along % 2), along)
    return core, along


def tile_order(near, order_ref):
    core, along = target_place(iota((NA, 256), 0))
    pick_rows = mask(iota((NA, 256), 1) == core * STRIDES["core"] + along * STRIDES["zh"] + own_part(BETA))
    wide = iota((256, PTS), 1)
    pick_cols = mask((iota((256, PTS), 0) == cluster_of(wide, BETA) + own_part(ALPHA)) & (wide < NB))
    listed = dot(dot(pick_rows, near, ((1,), (0,))).astype(bf16), pick_cols, ((1,), (0,))).astype(bf16)
    k = iota((PTS, TILES), 1)
    flat = dot(listed, mask(iota((PTS, TILES), 0) == k % NB), ((1,), (0,)))
    own = iota((NA, TILES), 1) // NB == iota((NA, TILES), 0)
    flat = jnp.sum(jnp.where(own, flat, 0.0), axis=0, keepdims=True)
    square = (TILES, TILES)
    before = mask(iota(square, 0) < iota(square, 1))
    place = dot(jnp.broadcast_to(flat, (8, TILES)).astype(bf16), before, ((1,), (0,)))[0:1]
    hit = mask((place.astype(i32) == iota(square, 0)) & (flat > 0.5))
    k = iota((8, TILES), 1)
    row = iota((8, TILES), 0)
    codes = jnp.where(row == 0, k // NB, jnp.where(row == 1, k % NB, 0)).astype(f32).astype(bf16)
    found = dot(codes, hit, ((1,), (1,))).astype(i32)
    count = jnp.sum(flat, axis=1, keepdims=True).astype(i32)
    entry = jnp.where(iota((1, TILES), 1) < count, found[0:1] * ROW + found[1:2], NB)
    order_ref[:, 0:TILES] = entry
    lane = iota((1, LIST - TILES), 1)
    order_ref[:, TILES:] = jnp.where(lane == LIST - TILES - 1, count, NB)


def parities():
    return lax.axis_index("core") % 2, lax.axis_index("zh") % 2, lax.axis_index("y") % 2


def order_kernel(near_ref, order_ref):
    tile_order(mask(near_ref[...] != 0), order_ref)


def prep_kernel(vol_ref, pts_ref, wts_ref, map_ref, tgt_ref, src_ref, vol_out, wts_out, map_out,
                xe_ref, xo_ref, ye_ref, yo_ref, ze_ref, zo_ref, scr):
    vol_out[...] = vol_ref[...]
    wts_out[...] = wts_ref[...]
    map_out[...] = map_ref[...]
    point_rows(pts_ref[...], scr, src_ref, tgt_ref)
    px, py, pz = parities()
    xe_ref[0:FACE, :] = vol_ref[:, 1 - px].reshape(FACE, CZ).astype(bf16)
    xe_ref[FACE:, :] = tgt_ref[...]
    xo_ref[...] = vol_ref[:, px].reshape(FACE, CZ).astype(bf16)
    low = vol_ref[:, :, 0, :].reshape(CH * CX, CZ).astype(bf16)
    high = vol_ref[:, :, CY - 1, :].reshape(CH * CX, CZ).astype(bf16)
    ye_ref[...] = jnp.where(py == 0, high, low)
    yo_ref[...] = jnp.where(py == 0, low, high)
    v = vol_ref[...].reshape(CH * CX * CY, CZ).astype(bf16)
    row, col = iota((HALO, CZ), 0), iota((HALO, CZ), 1)
    up = mask((row == 0) & (col == CZ - 1))
    down = mask((row == 1) & (col == 0))
    ze_ref[...] = dot(jnp.where(pz == 0, up, down), v, ((1,), (1,))).astype(bf16)
    zo_ref[...] = dot(jnp.where(pz == 0, down, up), v, ((1,), (1,))).astype(bf16)


def near_kernel(face_ref, own_ref, core_ref, out_ref):
    out_ref[0:SIDE, :] = face_ref[...]
    out_ref[SIDE : SIDE + BLOCK, :] = own_ref[...]
    out_ref[SIDE + BLOCK :, :] = core_ref[FACE:, :]


def far_kernel(own_ref, core_ref, pair_ref, out_ref):
    out_ref[0:BLOCK, :] = own_ref[...]
    out_ref[BLOCK : 2 * BLOCK, :] = core_ref[FACE:, :]
    out_ref[2 * BLOCK :, :] = pair_ref[SIDE:, :]


def relax_kernel(vol_ref, forc_ref, med_ref, xe_ref, xo_ref, ye_ref, yo_ref, ze_ref, zo_ref,
                 wts_ref, map_ref, src_ref, rel_ref, pack_ref):
    px, py, _ = parities()
    v = vol_ref[...]
    xe = xe_ref[0:FACE, :].astype(f32).reshape(CH, CY, CZ)
    xo = xo_ref[...].astype(f32).reshape(CH, CY, CZ)
    xl, xh = jnp.where(px == 0, xo, xe), jnp.where(px == 0, xe, xo)
    bx = jnp.stack([xl + v[:, 1], v[:, 0] + xh], axis=1)
    v3 = v.reshape(CH * CX, CY, CZ)
    row = iota(v3.shape, 1)
    ye, yo = ye_ref[0:SIDE, :].astype(f32), yo_ref[...].astype(f32)
    yl, yh = jnp.where(py == 0, yo, ye)[:, None, :], jnp.where(py == 0, ye, yo)[:, None, :]
    by = jnp.where(row == 0, yl, pltpu.roll(v3, 1, 1)) + jnp.where(row == CY - 1, yh, pltpu.roll(v3, CY - 1, 1))
    v2 = v.reshape(CH * CX * CY, CZ)
    lane = iota(v2.shape, 1)
    row, col = iota((HALO, CZ), 0), iota((HALO, CZ), 1)
    place = mask(((row == 0) & (col == 0)) | ((row == 1) & (col == CZ - 1)))
    zhalo = (ze_ref[...].astype(f32) + zo_ref[...].astype(f32)).astype(bf16)
    bz = (
        jnp.where(lane == 0, 0.0, pltpu.roll(v2, 1, 1))
        + jnp.where(lane == CZ - 1, 0.0, pltpu.roll(v2, CZ - 1, 1))
        + dot(zhalo, place, ((0,), (0,)))
    )
    beside = bx + by.reshape(v.shape) + bz.reshape(v.shape)
    a = med_ref[0]
    b = med_ref[1]
    lap = 6.0 * v - beside
    re, im = v[:RHS], v[RHS:]
    out_re = lap[:RHS] - a[None] * re + b[None] * im
    out_im = lap[RHS:] - a[None] * im - b[None] * re
    res = forc_ref[...] - jnp.concatenate([out_re, out_im], 0)
    rate = RELAX_RATE / (6.0 - a)
    relaxed = v + res * rate[None]
    rel_ref[...] = relaxed
    cells = map_ref[...]
    pick = mask(iota((CZ, PTS), 0) == cells % CZ)
    hi, mid, lo = split3(relaxed.reshape(CH * CX * CY, CZ))
    at = (
        dot(hi.astype(bf16), pick, ((1,), (0,)))
        + dot(mid.astype(bf16), pick, ((1,), (0,)))
        + dot(lo.astype(bf16), pick, ((1,), (0,)))
    )
    keep = (iota((CX * CY, PTS), 0) == cells // CZ).astype(f32)
    at = at.reshape(CH, CX * CY, PTS) * keep[None]
    traces = (jnp.sum(at, axis=1) * wts_ref[...]).astype(bf16)
    pack_ref[:, 0:BLOCK, :] = jnp.broadcast_to(src_ref[...][None], (NB, BLOCK, PTS))
    pack_ref[:, BLOCK:, :] = jnp.broadcast_to(traces[None], (NB, CH, PTS))


def evaluate(dist2):
    inv = lax.rsqrt(dist2)
    turns = dist2 * inv
    f = turns - jnp.round(turns)
    z = f * f
    s = f * ((S2 * z + S1) * z + S0)
    a = s * s
    c2 = RT2 - a
    w = LAM2 - a
    c = w * lax.rsqrt(w)
    s2 = s * c
    over = SCALE * inv
    e = s2 * over
    return (over - e * s2).astype(bf16), (e * c2).astype(bf16)


def pair_kernel(order_ref, pack_ref, near_ref, far_ref, out_ref, sum_ref, a_ref, b_ref, w_ref, d0, d1, g0, g1):
    sum_ref[...] = jnp.zeros_like(sum_ref)
    to_source = chooser((BLOCK, EXT), 1, SOURCE_ROWS)
    to_target = chooser((EXT, BLOCK), 0, TARGET_ROWS)
    for i in range(NA):
        ref = near_ref if i < NA // 2 else far_ref
        start = i % (NA // 2) * BLOCK
        b_ref[i] = dot(to_target, ref[start : start + BLOCK, :], ((1,), (0,))).astype(bf16)
    for j in range(NB):
        a_ref[j] = dot(pack_ref[j, 0:BLOCK, :], to_source, ((0,), (0,))).astype(bf16)
        t = pack_ref[j, BLOCK:, :]
        w_ref[j, :, 0:PTS] = t
        w_ref[j, :, PTS:] = jnp.concatenate([-t[RHS:], t[:RHS]], 0)
    a_ref[NB] = a_ref[0]
    w_ref[NB] = jnp.zeros((CH, 2 * PTS), bf16)
    pairs = (order_ref[LIST - 1] + (2 * NT - 1)) // (2 * NT)

    def code(group, q):
        c = order_ref[group * NT + q]
        return c >> 6, c & (ROW - 1)

    def dist(group, d_ref, q):
        i, j = code(group, q)
        d_ref[q] = jnp.dot(a_ref[j], b_ref[i], preferred_element_type=f32)

    def add(group, g_ref, q):
        i, j = code(group, q)
        sum_ref[i] += jnp.dot(w_ref[j], g_ref[q], preferred_element_type=f32)

    def values(d_ref, g_ref, q):
        re, im = evaluate(d_ref[q])
        g_ref[q, 0:PTS, :] = re
        g_ref[q, PTS:, :] = im

    for q in range(NT):
        dist(0, d0, q)
    g1[...] = jnp.zeros_like(g1)

    def body(k, _):
        for q in range(NT):
            dist(2 * k + 1, d1, q)
            values(d0, g0, q)
            add(jnp.maximum(2 * k - 1, 0), g1, q)
        for q in range(NT):
            dist(2 * k + 2, d0, q)
            values(d1, g1, q)
            add(2 * k, g0, q)
        return 0

    lax.fori_loop(0, pairs, body, 0)
    for q in range(NT):
        add(jnp.maximum(2 * pairs - 1, 0), g1, q)
    for i in range(NA):
        core, along = target_place(jnp.int32(i))
        out_ref[core * SIZES["zh"] + along] = sum_ref[i].astype(bf16)


def finish_kernel(part_ref, rel_ref, map_ref, new_ref, pot_ref):
    pot = jnp.sum(part_ref[...].astype(f32), axis=0)
    pot_ref[...] = pot
    cells = map_ref[...]
    keep = (iota((CX * CY, PTS), 0) == cells // CZ).astype(f32)
    pick = mask(iota((CZ, PTS), 0) == cells % CZ)
    spread = jnp.zeros((CH * CX * CY, CZ), f32)
    for part in split3(pot * COUPLING):
        wide = (part[:, None, :] * keep[None]).reshape(CH * CX * CY, PTS).astype(bf16)
        spread = spread + dot(wide, pick, ((1,), (1,)))
    new_ref[...] = rel_ref[...] + spread.reshape(CH, CX, CY, CZ)


def call(kernel, args, spaces, outs, kept, scratch=()):
    args = [pltpu.with_memory_space_constraint(a, pltpu.VMEM) if c == "v" else a for a, c in zip(args, spaces)]
    return pl.pallas_call(
        kernel,
        out_shape=[
            (pltpu.VMEM if c == "v" else jax.ShapeDtypeStruct)(shape, dtype) for (shape, dtype), c in zip(outs, kept)
        ],
        in_specs=[pl.BlockSpec(memory_space=pltpu.SMEM if c == "s" else pltpu.VMEM) for c in spaces],
        out_specs=[pl.BlockSpec(memory_space=pltpu.VMEM)] * len(outs),
        scratch_shapes=[pltpu.VMEM(shape, dtype) for shape, dtype in scratch],
    )(*args)


def swap(x, axes, parity):
    size = math.prod(SIZES[a] for a in axes)
    pairs = [q for k in range(parity, size - 1, 2) for q in ((k, k + 1), (k + 1, k))]
    return lax.ppermute(x, axes if len(axes) > 1 else axes[0], pairs)


def sweep(volume, forcing, medium, points, weights, cell_map, near_list):
    tgt, src, vol, wts, cells, xe, xo, ye, yo, ze, zo = call(
        prep_kernel,
        (volume, points, weights[None, :], cell_map[None, :]),
        "hhhh",
        [((BLOCK, PTS), bf16), ((BLOCK, PTS), bf16), ((CH, CX, CY, CZ), f32), ((1, PTS), f32), ((1, PTS), i32)]
        + [((rows, CZ), bf16) for rows in (FACE + BLOCK, FACE, SIDE, SIDE)]
        + [((HALO, CH * CX * CY), bf16)] * 2,
        "v" * 11,
        [((BLOCK, PTS), f32)],
    )
    xe = swap(xe, GRP, 0)
    xo = swap(xo, GRP, 1)
    yo = swap(yo, ("zh",), 1)
    ze = swap(ze, ("y",), 0)
    zo = swap(zo, ("y",), 1)
    (ye,) = call(near_kernel, (ye, tgt, xe), "vvv", [((SIDE + 2 * BLOCK, PTS), bf16)], "v")
    ye = swap(ye, ("zh",), 0)
    (quad,) = call(far_kernel, (tgt, xe, ye), "vvv", [((4 * BLOCK, PTS), bf16)], "v")
    mirror = [(k, SIZES["zh"] - 1 - k) for k in range(SIZES["zh"])]
    far = lax.ppermute(quad, "zh", mirror)
    relaxed, pack = call(
        relax_kernel,
        (vol, forcing, medium, xe, xo, ye, yo, ze, zo, wts, cells, src),
        "v" * 12,
        [((CH, CX, CY, CZ), f32), ((NB, BLOCK + CH, PTS), bf16)],
        "vv",
    )
    packs = lax.all_to_all(pack, BETA, 0, 0, tiled=True)
    (order,) = call(order_kernel, (near_list,), "v", [((1, LIST), i32)], "h")
    order = order.reshape(LIST)
    (part,) = call(
        pair_kernel,
        (order, packs, quad, far),
        "svvv",
        [((NA, CH, PTS), bf16)],
        "v",
        [
            ((NA, CH, PTS), f32),
            ((NB + 1, PTS, EXT), bf16),
            ((NA, EXT, PTS), bf16),
            ((NB + 1, CH, 2 * PTS), bf16),
            ((NT, PTS, PTS), f32),
            ((NT, PTS, PTS), f32),
            ((NT, 2 * PTS, PTS), bf16),
            ((NT, 2 * PTS, PTS), bf16),
        ],
    )
    parts = lax.all_to_all(part, ALPHA, 0, 0, tiled=True)
    new_volume, potential = call(
        finish_kernel, (parts, relaxed, cells), "vvv", [((CH, CX, CY, CZ), f32), ((CH, PTS), f32)], "hh"
    )
    return new_volume, potential


def solution(mesh):
    split = Mesh(np.asarray(mesh.devices).reshape([SIZES[a] for a in AXES]), AXES)
    grid = P(None, ("x", "zl", "core"), "zh", "y")
    return jax.shard_map(
        sweep,
        mesh=split,
        in_specs=(grid, grid, grid, P(None, AXES), P(AXES), P(AXES), P()),
        out_specs=(grid, P(None, AXES)),
        check_vma=False,
    )
```
